32 devices in a mesh: grp: 2 (over y), tile: 4 (over z), rep: 4 (over x, core).
Axes of the slice: x: 2, y: 2, z: 4, core: 2. Of those that a mesh axis runs over, the one named last changes fastest.
Arguments:
- focusing: bfloat16 [2, 512, 1024], P(None, 'grp', 'tile'), parts along dimension 1, may hold values from -6 to 6
- source_basis: bfloat16 [2, 64, 8, 1024], P(None, 'rep', 'grp', 'tile'), parts along dimension 2, may hold values from -0.375 to 0.375
- receiver_basis: bfloat16 [2, 64, 8, 1024], P(None, 'rep', 'grp', 'tile'), parts along dimension 2, may hold values from -0.21875 to 0.21875
- tile_ranks: int32 [8, 4], P('grp', 'tile'), parts along dimension 0, may hold values from 1 to 4
- keep_counts: int32 [8], P(('grp', 'tile')), parts along dimension 0, may hold values from 64 to 256
Outputs:
- forward_data: float32 [2, 512, 1024], P(None, ('grp', 'rep'), 'tile'), parts along dimension 1
- muted_adjoint_result: float32 [2, 512, 1024], P(None, ('grp', 'rep'), 'tile'), parts along dimension 1
- correlations: float32 [2, 256, 512], P(None, 'rep', 'grp'), parts along dimension 2
The draws below stay inside these ranges and needn't reach their ends.
There are 2 independent parts, one for each index of `grp`. The reference program is written for one: setup_inputs(seed, part) draws one part's arguments, and reference() takes and returns one part's arrays. A program takes and returns all parts, laid end to end along the dimension named above; each array names one. Nothing has to cross between parts.
Inputs may be any that keep to these rules, and one draw needn't show every extreme that they name: `tile_ranks`: number of live buckets of 16 ranks in each tile. `keep_counts`: receivers kept in each receiver tile, counted from its first position.
All inputs are finite; a program needn't handle non-finite values.
Results may differ from the reference program's by a relative error of at most 0.0039.
Values may be sent and summed in bfloat16 or wider, within the bound.
No kernel may reach another device: no remote copies, remote signals or barrier semaphores. Data moves between devices by JAX's collectives and lax.ppermute only.
A program may use at most 64 MiB of HBM per device.

```python
import math
import jax
import jax.numpy as jnp
from jax import lax

SPAN = 256
RMAX = 64
BUCKET = 16
FOC = 256
TILES = 4
NS = 1024


def touch_ends(values, own_key, low, largest):
    spot = [jax.random.randint(jax.random.fold_in(own_key, axis), (), 0, length) for axis, length in enumerate(values.shape)]
    main_axis = values.shape.index(max(values.shape))
    beside = spot[:main_axis] + [(spot[main_axis] + 1) % values.shape[main_axis]] + spot[main_axis + 1:]
    return values.at[tuple(spot)].set(low).at[tuple(beside)].set(largest)


def shard_levels(rng, shape, split, smallest, largest):
    gain = 1.0
    for position, parts in split:
        heights = jax.random.uniform(jax.random.fold_in(jax.random.fold_in(rng, 6), position), (parts,), jnp.float32, smallest / len(split), largest / len(split))
        gain = gain * jnp.repeat(jnp.exp(heights), shape[position] // parts).reshape((-1,) + (1,) * (len(shape) - 1 - position))
    return gain


def centred(key, dims, width, bound, pieces=(), held_as=jnp.bfloat16):
    result = width * jax.random.normal(key, dims, jnp.float32)
    if pieces:
        result = result * shard_levels(key, dims, pieces, -0.22, 0.18)
    return jnp.clip(result, -bound, bound).astype(held_as)


def setup_inputs(seed: int = 0, part: int = 0) -> dict:
    seeds = jax.random.split(jax.random.key(seed), 6)
    own_keys = jax.random.split(jax.random.fold_in(seeds[5], part), 6)
    focusing = centred(own_keys[0], (2, FOC, NS), 1.0, 6.0, ((2, 4),))
    source_basis = centred(own_keys[1], (2, RMAX, TILES, NS), SPAN ** -0.5, 0.375, ((1, 4), (3, 4)))
    receiver_basis = centred(own_keys[2], (2, RMAX, TILES, NS), (3 * RMAX * TILES) ** -0.5, 0.21875, ((1, 4), (3, 4)))
    tile_ranks = touch_ends(jax.random.randint(own_keys[3], (TILES, TILES), 1, RMAX // BUCKET + 1), jax.random.fold_in(own_keys[3], 1), 1, (RMAX // BUCKET + 1) - 1).astype(jnp.int32)
    keep_counts = touch_ends(jax.random.randint(own_keys[4], (TILES,), SPAN // 4, SPAN + 1), jax.random.fold_in(own_keys[4], 1), SPAN // 4, SPAN).astype(jnp.int32)
    return dict(focusing=focusing, source_basis=source_basis, receiver_basis=receiver_basis, tile_ranks=tile_ranks, keep_counts=keep_counts)


def reference(focusing, source_basis, receiver_basis, tile_ranks, keep_counts):
    bucket_index = jnp.arange(RMAX, dtype=jnp.int32) // BUCKET
    live_all = bucket_index[:, None, None] < tile_ranks[None, :, :]
    focal_wide = focusing.astype(jnp.float32)

    def forward_column(running, column):
        first_cell = (column * SPAN).astype(jnp.int32)
        basis_column_vector = lax.dynamic_slice_in_dim(source_basis, first_cell, SPAN, 3).astype(jnp.float32)
        focal_col = lax.dynamic_slice_in_dim(focal_wide, first_cell, SPAN, 2)
        blocks = jnp.einsum('pkas,qfs->pqkaf', basis_column_vector, focal_col)
        live_col = lax.dynamic_index_in_dim(live_all, column, 2, keepdims=False)
        stacked = jnp.stack([blocks[0, 0] - blocks[1, 1], blocks[0, 1] + blocks[1, 0]])
        rounded = jnp.where(live_col[None, :, :, None], stacked, 0.0).astype(jnp.bfloat16)
        coefficient = lax.optimization_barrier(rounded).astype(jnp.float32)
        lifting = lax.dynamic_index_in_dim(receiver_basis, column, 2, keepdims=False)
        lifting = lifting.astype(jnp.float32).reshape(2, RMAX, TILES, SPAN)
        blocks = jnp.einsum('pkaf,qkar->pqfar', coefficient, lifting)
        return (running + jnp.stack([blocks[0, 0] - blocks[1, 1], blocks[1, 0] + blocks[0, 1]]), None)
    columns_all = jnp.arange(TILES, dtype=jnp.int32)
    start_value = jnp.zeros((2, FOC, TILES, SPAN), jnp.float32)
    forward_grid, unused = lax.scan(forward_column, start_value, columns_all)
    forward_data = forward_grid.reshape(2, FOC, NS)
    weights = (jnp.arange(SPAN, dtype=jnp.int32)[None, :] < keep_counts[:, None]).astype(jnp.float32).reshape(NS)
    masked = (forward_data * weights).astype(jnp.bfloat16)
    masked_wide = lax.optimization_barrier(masked).astype(jnp.float32).reshape(2, FOC, TILES, SPAN)

    def adjoint_column(running, column):
        first_cell = (column * SPAN).astype(jnp.int32)
        lifting = lax.dynamic_index_in_dim(receiver_basis, column, 2, keepdims=False)
        lifting = lifting.astype(jnp.float32).reshape(2, RMAX, TILES, SPAN)
        blocks = jnp.einsum('pkar,qfar->pqkaf', lifting, masked_wide)
        stacked = jnp.stack([blocks[0, 0] + blocks[1, 1], blocks[0, 1] - blocks[1, 0]])
        live_col = lax.dynamic_index_in_dim(live_all, column, 2, keepdims=False)
        rounded = jnp.where(live_col[None, :, :, None], stacked, 0.0).astype(jnp.bfloat16)
        coefficient = lax.optimization_barrier(rounded).astype(jnp.float32)
        basis_column_vector = lax.dynamic_slice_in_dim(source_basis, first_cell, SPAN, 3).astype(jnp.float32)
        blocks = jnp.einsum('pkaf,qkas->pqfs', coefficient, basis_column_vector)
        return (running, jnp.stack([blocks[0, 0] + blocks[1, 1], blocks[1, 0] - blocks[0, 1]]))
    unused_two, image_cols = lax.scan(adjoint_column, jnp.zeros((), jnp.float32), columns_all)
    muted_adjoint_result = jnp.transpose(image_cols, (1, 2, 0, 3)).reshape(2, FOC, NS)
    blocks = jnp.einsum('pgs,qfs->pqgf', muted_adjoint_result, focal_wide, precision=lax.Precision.HIGHEST)
    factor = 1.0 / math.sqrt(SPAN * NS)
    correlations = factor * jnp.stack([blocks[0, 0] + blocks[1, 1], blocks[1, 0] - blocks[0, 1]])
    return (forward_data, muted_adjoint_result, correlations)
```

```python
import functools
import math

import jax
import jax.numpy as jnp
from jax import lax
from jax.experimental import pallas as pl
from jax.experimental.pallas import tpu as pltpu
from jax.sharding import PartitionSpec as P


SPAN = 256
BUCKET = 16
BF16 = jnp.bfloat16
F32 = jnp.float32

NT = (((1,), (1,)), ((), ()))
NN = (((1,), (0,)), ((), ()))
TN = (((0,), (0,)), ((), ()))


def dot(a, b, dims):
    return lax.dot_general(a, b, dims, preferred_element_type=F32)


def swap(x, axis, step):
    count = lax.axis_size(axis)
    return lax.ppermute(x, axis, [(i, i ^ step) for i in range(count)])


LANES = 128


def fold(ref, start, value):
    rows, columns = value.shape
    for part in range(columns // LANES):
        ref[part, pl.ds(start, rows), :] = value[:, part * LANES : (part + 1) * LANES]


def every(ref, start, count, stride):
    parts = [ref[part, pl.ds(start, count, stride=stride), :] for part in range(ref.shape[0])]
    return jnp.concatenate(parts, axis=1)


def live_rows(ranks_ref, cell, shard, ranks):
    rows = lax.broadcasted_iota(jnp.int32, (ranks, 1), 0) + shard * ranks
    return rows < ranks_ref[cell, 0] * BUCKET


def forward_kernel(ranks_ref, basis_ref, foc_ref, *refs, tiles, ranks):
    outs, made, blocks = refs[:tiles], refs[tiles], refs[tiles + 1]
    here = lax.axis_index("tile")
    shard = lax.axis_index("rep")
    half = ranks * tiles
    points = foc_ref.shape[0] // 2
    prod = dot(basis_ref[...], foc_ref[...], NT)
    fold(made, 0, prod[:half, :points] - prod[half:, points:])
    fold(made, half, prod[:half, points:] + prod[half:, :points])
    for cell in range(tiles):
        mask = live_rows(ranks_ref, cell, shard, ranks)
        for part in range(2):
            rows = every(made, part * half + cell, ranks, tiles)
            blocks[cell, pl.ds(part * ranks, ranks), :] = jnp.where(mask, rows, 0.0).astype(BF16)
    for step in range(tiles):
        outs[step][...] = blocks[here ^ step]


def lift_kernel(keep_ref, *refs, tiles, reps, ranks):
    pieces, out, weight, wide = refs[:reps], refs[reps], refs[reps + 1], refs[reps + 2]
    here = lax.axis_index("tile")
    half = ranks * tiles
    width = pieces[0].shape[1]
    columns = lax.broadcasted_iota(jnp.int32, weight.shape, 1)
    columns = jnp.where(columns >= width, columns - width, columns)
    weight[...] = (columns < keep_ref[0]).astype(F32)
    for shard in range(reps):
        fold(wide, 0, pieces[shard][...].astype(F32))
        for cell in range(tiles):
            real = every(wide, cell, ranks, tiles)
            imag = every(wide, half + cell, ranks, tiles)
            spot = here ^ cell
            out[spot, shard, pl.ds(0, ranks), pl.ds(0, width)] = real.astype(BF16)
            out[spot, shard, pl.ds(0, ranks), pl.ds(width, width)] = imag.astype(BF16)
            out[spot, shard, pl.ds(ranks, ranks), pl.ds(0, width)] = (-imag).astype(BF16)
            out[spot, shard, pl.ds(ranks, ranks), pl.ds(width, width)] = real.astype(BF16)


def image_basis_kernel(ranks_ref, *refs, tiles, reps, ranks):
    pieces, out, wide = refs[:reps], refs[reps], refs[reps + 1]
    here = lax.axis_index("tile")
    me = lax.axis_index("rep")
    half = ranks * tiles
    width = pieces[0].shape[1]
    for shard in range(reps):
        fold(wide, 0, pieces[shard][...].astype(F32))
        for cell in range(tiles):
            mask = live_rows(ranks_ref, cell, me ^ shard, ranks)
            real = jnp.where(mask, every(wide, cell, ranks, tiles), 0.0)
            imag = jnp.where(mask, every(wide, half + cell, ranks, tiles), 0.0)
            spot = here ^ cell
            out[spot, shard, pl.ds(0, ranks), pl.ds(0, width)] = real.astype(BF16)
            out[spot, shard, pl.ds(0, ranks), pl.ds(width, width)] = (-imag).astype(BF16)
            out[spot, shard, pl.ds(ranks, ranks), pl.ds(0, width)] = imag.astype(BF16)
            out[spot, shard, pl.ds(ranks, ranks), pl.ds(width, width)] = real.astype(BF16)


def middle_kernel(*refs, tiles, reps, factor):
    pieces, lift_ref, weight_ref = refs[:reps], refs[reps], refs[reps + 1]
    fwd_out, own_corr, own_back = refs[reps + 2], refs[reps + 3], refs[reps + 4]
    sends, whole = refs[reps + 5 : reps + 4 + tiles], refs[reps + 4 + tiles]
    me = lax.axis_index("rep")
    points, width2 = whole.shape
    width = width2 // 2
    share = points // reps
    block = lift_ref.shape[2]
    total = None
    for shard in range(reps):
        lift = lift_ref[:, shard].reshape(tiles * block, width2)
        part = dot(pieces[shard][...], lift, TN)
        total = part if total is None else total + part
    whole[...] = total
    mine = whole[pl.ds(pl.multiple_of(me * share, share), share), :]
    fwd_out[0] = mine[:, :width]
    fwd_out[1] = mine[:, width:]
    muted = (mine * weight_ref[pl.ds(0, 1), :]).astype(BF16)
    back = dot(muted, lift_ref[...].reshape(tiles * reps * block, width2), NT).astype(BF16)
    cell = reps * block
    high = total.astype(BF16)
    low = (total - high.astype(F32)).astype(BF16)
    turned = jnp.concatenate([muted[:, width:], -muted[:, :width]], axis=1)
    left = jnp.concatenate([muted, turned], axis=0)
    corr = (dot(left, high, NT) + dot(left, low, NT)) * factor
    own_corr[...] = corr
    own_back[...] = back[:, :cell]
    small = corr.astype(BF16)
    for step in range(1, tiles):
        out = sends[step - 1]
        out[pl.ds(0, 2 * share), :] = small
        piece = back[:, step * cell : (step + 1) * cell]
        out[pl.ds(2 * share, share // 2), pl.ds(0, cell)] = piece[: share // 2]
        out[pl.ds(2 * share, share // 2), pl.ds(cell, cell)] = piece[share // 2 :]


def final_kernel(*refs, tiles, reps):
    own_corr, own_back, basis_ref = refs[:3]
    arrived = refs[3 : 2 + tiles]
    adj_out, corr_out, back = refs[2 + tiles :]
    share = own_back.shape[0]
    cell = own_back.shape[1]
    width2 = basis_ref.shape[3]
    width = width2 // 2
    block = basis_ref.shape[2]
    back[:, pl.ds(0, cell)] = own_back[...]
    corr = own_corr[...]
    for step in range(1, tiles):
        got = arrived[step - 1]
        corr = corr + got[pl.ds(0, 2 * share), :].astype(F32)
        back[pl.ds(0, share // 2), pl.ds(step * cell, cell)] = got[pl.ds(2 * share, share // 2), pl.ds(0, cell)]
        back[pl.ds(share // 2, share // 2), pl.ds(step * cell, cell)] = got[pl.ds(2 * share, share // 2), pl.ds(cell, cell)]
    image = dot(back[...], basis_ref[...].reshape(tiles * reps * block, width2), NN)
    adj_out[0] = image[:, :width]
    adj_out[1] = image[:, width:]
    corr_out[0] = corr[:share]
    corr_out[1] = corr[share:]


def call(kernel, ins, outs, scratch, args):
    vmem, smem = pl.BlockSpec(memory_space=pltpu.VMEM), pl.BlockSpec(memory_space=pltpu.SMEM)
    return pl.pallas_call(
        kernel,
        in_specs=[smem if kind == "s" else vmem for kind in ins],
        out_specs=jax.tree.map(lambda _: vmem, outs),
        out_shape=outs,
        scratch_shapes=scratch,
    )(*args)


def short_path(focusing, source_basis, receiver_basis, tile_ranks, keep_counts):
    tiles, reps = lax.axis_size("tile"), lax.axis_size("rep")
    ranks, width = source_basis.shape[1], source_basis.shape[3]
    points = focusing.shape[1]
    share = points // reps
    block = 2 * ranks
    factor = 1.0 / math.sqrt(SPAN * width * tiles)
    shaped = jax.ShapeDtypeStruct
    order = sorted(range(1, tiles), reverse=True)
    rep_order = sorted(range(1, reps), key=lambda s: (s == 1, s))

    source = source_basis.reshape(2 * ranks * tiles, width)
    receiver = receiver_basis.reshape(2 * ranks * tiles, width)
    made = call(
        functools.partial(forward_kernel, tiles=tiles, ranks=ranks),
        "svv",
        [shaped((block, points), BF16)] * tiles,
        [pltpu.VMEM((points // LANES, block * tiles, LANES), F32), pltpu.VMEM((tiles, block, points), BF16)],
        (tile_ranks, source, focusing.reshape(2 * points, width)),
    )
    got = {step: swap(made[step], "tile", step) for step in order}
    lifts = {step: swap(receiver, "rep", step) for step in rep_order}
    gathered = jnp.concatenate([made[0]] + [got[step] for step in range(1, tiles)], axis=0)
    spread = {step: swap(gathered, "rep", step) for step in rep_order}
    lift, weight = call(
        functools.partial(lift_kernel, tiles=tiles, reps=reps, ranks=ranks),
        "s" + "v" * reps,
        [shaped((tiles, reps, block, 2 * width), BF16), shaped((8, 2 * width), F32)],
        [pltpu.VMEM((width // LANES, block * tiles, LANES), F32)],
        (keep_counts, receiver, *[lifts[step] for step in range(1, reps)]),
    )
    middle = call(
        functools.partial(middle_kernel, tiles=tiles, reps=reps, factor=factor),
        "v" * (reps + 2),
        [shaped((2, share, width), F32), shaped((2 * share, points), F32), shaped((share, reps * block), BF16)]
        + [shaped((2 * share + share // 2, points), BF16)] * (tiles - 1),
        [pltpu.VMEM((points, 2 * width), F32)],
        (gathered, *[spread[step] for step in range(1, reps)], lift, weight),
    )
    forward_data, own_corr, own_back = middle[:3]
    sent = {step: swap(middle[2 + step], "tile", step) for step in order}
    bases = {step: swap(source, "rep", step) for step in rep_order}
    basis = call(
        functools.partial(image_basis_kernel, tiles=tiles, reps=reps, ranks=ranks),
        "s" + "v" * reps,
        shaped((tiles, reps, block, 2 * width), BF16),
        [pltpu.VMEM((width // LANES, block * tiles, LANES), F32)],
        (tile_ranks, source, *[bases[step] for step in range(1, reps)]),
    )
    adjoint, corr = call(
        functools.partial(final_kernel, tiles=tiles, reps=reps),
        "v" * (tiles + 2),
        [shaped((2, share, width), F32), shaped((2, share, points), F32)],
        [pltpu.VMEM((share, tiles * reps * block), BF16)],
        (own_corr, own_back, basis, *[sent[step] for step in range(1, tiles)]),
    )
    return forward_data, adjoint, corr


def bucket_live(rank_column, ranks):
    return (lax.iota(jnp.int32, ranks) // BUCKET)[:, None] < rank_column[None, :]


def long_path(focusing, source_basis, receiver_basis, tile_ranks, keep_counts):
    width = focusing.shape[2]
    share = focusing.shape[1] // lax.axis_size("rep")
    weights = (lax.iota(jnp.int32, width) < keep_counts[0]).astype(F32)
    factor = 1.0 / math.sqrt(SPAN * width * lax.axis_size("tile"))
    source = lax.all_gather(source_basis, "rep", axis=1, tiled=True)
    receiver = lax.all_gather(receiver_basis, "rep", axis=1, tiled=True)
    focal = lax.dynamic_slice_in_dim(focusing, lax.axis_index("rep") * share, share, 1)
    ranks, cells = source.shape[1], source.shape[2]
    live = bucket_live(tile_ranks[:, 0], ranks)

    blocks = dot(source.reshape(-1, width), focal.reshape(-1, width), NT)
    blocks = blocks.reshape(2, ranks, cells, 2, share)
    coef = jnp.stack([blocks[0, :, :, 0] - blocks[1, :, :, 1], blocks[0, :, :, 1] + blocks[1, :, :, 0]])
    coef = jnp.where(live[None, :, :, None], coef, 0.0).astype(BF16)[:, :, :, None]
    coef = lax.all_to_all(coef, "tile", split_axis=2, concat_axis=3, tiled=True)
    coef = coef.reshape(2, ranks * cells, share)
    flat = receiver.reshape(2, ranks * cells, width)
    blocks = jnp.einsum("wgh,lgj->wlhj", coef, flat, preferred_element_type=F32)
    forward_data = jnp.stack([blocks[0, 0] - blocks[1, 1], blocks[1, 0] + blocks[0, 1]])
    masked = (forward_data * weights).astype(BF16)

    blocks = jnp.einsum("pks,qfs->pqkf", flat, masked, preferred_element_type=F32)
    back = jnp.stack([blocks[0, 0] + blocks[1, 1], blocks[0, 1] - blocks[1, 0]]).astype(BF16)
    back = back.reshape(2, ranks, 1, cells, share)
    back = lax.all_to_all(back, "tile", split_axis=3, concat_axis=2, tiled=True)
    back = jnp.where(live[None, :, :, None, None], back, jnp.zeros((), BF16)).reshape(2, ranks * cells, share)
    flat = source.reshape(2, ranks * cells, width)
    blocks = jnp.einsum("wgh,lgj->wlhj", back, flat, preferred_element_type=F32)
    adjoint = jnp.stack([blocks[0, 0] + blocks[1, 1], blocks[1, 0] - blocks[0, 1]])
    blocks = jnp.einsum(
        "pgs,qfs->pqgf", adjoint, focusing.astype(F32), precision=lax.Precision.HIGHEST, preferred_element_type=F32
    )
    corr = factor * jnp.stack([blocks[0, 0] + blocks[1, 1], blocks[1, 0] - blocks[0, 1]])
    return forward_data, adjoint, lax.psum(corr, "tile")


def power_of_two(n):
    return n & (n - 1) == 0


def solution(mesh):
    tiles, reps = mesh.shape["tile"], mesh.shape["rep"]
    short = tiles <= 4 and power_of_two(tiles) and power_of_two(reps)

    def per_device(*args):
        return (short_path if short else long_path)(*args)

    placed = (
        P(None, "grp", "tile"),
        P(None, "rep", "grp", "tile"),
        P(None, "rep", "grp", "tile"),
        P("grp", "tile"),
        P(("grp", "tile")),
    )
    return jax.shard_map(
        per_device,
        mesh=mesh,
        in_specs=placed,
        out_specs=(P(None, ("grp", "rep"), "tile"), P(None, ("grp", "rep"), "tile"), P(None, "rep", "grp")),
        check_vma=False,
    )
```

```python
import functools
import math

import jax
import jax.numpy as jnp
from jax import lax
from jax.experimental import pallas as pl
from jax.experimental.pallas import tpu as pltpu
from jax.sharding import PartitionSpec as P


SPAN = 256
BUCKET = 16
BF16 = jnp.bfloat16
F32 = jnp.float32

NT = (((1,), (1,)), ((), ()))
NN = (((1,), (0,)), ((), ()))
TN = (((0,), (0,)), ((), ()))


def dot(a, b, dims):
    return lax.dot_general(a, b, dims, preferred_element_type=F32)


def swap(x, axis, step):
    count = lax.axis_size(axis)
    return lax.ppermute(x, axis, [(i, i ^ step) for i in range(count)])


def live_rows(ranks_ref, cell, shard, ranks):
    rows = lax.broadcasted_iota(jnp.int32, (ranks, 1), 0) + shard * ranks
    return rows < ranks_ref[cell] * BUCKET


def forward_kernel(ranks_ref, basis_ref, foc_ref, *refs):
    ranks, tiles = basis_ref.shape[1], basis_ref.shape[2]
    outs, blocks = refs[:tiles], refs[tiles]
    here = lax.axis_index("tile")
    shard = lax.axis_index("rep")
    points = foc_ref.shape[0] // 2
    rows = [basis_ref[part, :, cell, :] for cell in range(tiles) for part in range(2)]
    prod = dot(jnp.concatenate(rows, axis=0), foc_ref[...], NT)
    for cell in range(tiles):
        mask = live_rows(ranks_ref, cell, shard, ranks)
        real = prod[2 * cell * ranks : (2 * cell + 1) * ranks]
        imag = prod[(2 * cell + 1) * ranks : (2 * cell + 2) * ranks]
        coef = [real[:, :points] - imag[:, points:], real[:, points:] + imag[:, :points]]
        for part in range(2):
            blocks[cell, pl.ds(part * ranks, ranks), :] = jnp.where(mask, coef[part], 0.0).astype(BF16)
    for step in range(tiles):
        outs[step][...] = blocks[here ^ step]


def lift_kernel(keep_ref, *refs, reps):
    pieces, out, weight = refs[:reps], refs[reps], refs[reps + 1]
    ranks, tiles, width = pieces[0].shape[1:]
    here = lax.axis_index("tile")
    columns = lax.broadcasted_iota(jnp.int32, weight.shape, 1)
    columns = jnp.where(columns >= width, columns - width, columns)
    weight[...] = (columns < keep_ref[0]).astype(F32)
    for shard in range(reps):
        for cell in range(tiles):
            real = pieces[shard][0, :, cell, :]
            imag = pieces[shard][1, :, cell, :]
            spot = here ^ cell
            out[spot, shard, pl.ds(0, ranks), pl.ds(0, width)] = real
            out[spot, shard, pl.ds(0, ranks), pl.ds(width, width)] = imag
            out[spot, shard, pl.ds(ranks, ranks), pl.ds(0, width)] = -imag
            out[spot, shard, pl.ds(ranks, ranks), pl.ds(width, width)] = real


def image_basis_kernel(ranks_ref, *refs, reps):
    pieces, out = refs[:reps], refs[reps]
    ranks, tiles, width = pieces[0].shape[1:]
    here = lax.axis_index("tile")
    me = lax.axis_index("rep")
    for shard in range(reps):
        for cell in range(tiles):
            mask = live_rows(ranks_ref, cell, me ^ shard, ranks)
            real = jnp.where(mask, pieces[shard][0, :, cell, :].astype(F32), 0.0)
            imag = jnp.where(mask, pieces[shard][1, :, cell, :].astype(F32), 0.0)
            spot = here ^ cell
            out[spot, shard, pl.ds(0, ranks), pl.ds(0, width)] = real.astype(BF16)
            out[spot, shard, pl.ds(0, ranks), pl.ds(width, width)] = (-imag).astype(BF16)
            out[spot, shard, pl.ds(ranks, ranks), pl.ds(0, width)] = imag.astype(BF16)
            out[spot, shard, pl.ds(ranks, ranks), pl.ds(width, width)] = real.astype(BF16)


def middle_kernel(*refs, tiles, reps, factor):
    pieces, lift_ref, weight_ref = refs[:reps], refs[reps], refs[reps + 1]
    fwd_out, own_corr, own_back = refs[reps + 2], refs[reps + 3], refs[reps + 4]
    sends, whole = refs[reps + 5 : reps + 4 + tiles], refs[reps + 4 + tiles]
    me = lax.axis_index("rep")
    points, width2 = whole.shape
    width = width2 // 2
    share = points // reps
    block = lift_ref.shape[2]
    total = None
    for shard in range(reps):
        lift = lift_ref[:, shard].reshape(tiles * block, width2)
        part = dot(pieces[shard][...], lift, TN)
        total = part if total is None else total + part
    whole[...] = total
    mine = whole[pl.ds(pl.multiple_of(me * share, share), share), :]
    fwd_out[0] = mine[:, :width]
    fwd_out[1] = mine[:, width:]
    muted = (mine * weight_ref[pl.ds(0, 1), :]).astype(BF16)
    back = dot(muted, lift_ref[...].reshape(tiles * reps * block, width2), NT).astype(BF16)
    cell = reps * block
    high = total.astype(BF16)
    low = (total - high.astype(F32)).astype(BF16)
    turned = jnp.concatenate([muted[:, width:], -muted[:, :width]], axis=1)
    left = jnp.concatenate([muted, turned], axis=0)
    corr = (dot(left, high, NT) + dot(left, low, NT)) * factor
    own_corr[...] = corr
    own_back[...] = back[:, :cell]
    small = corr.astype(BF16)
    for step in range(1, tiles):
        out = sends[step - 1]
        out[pl.ds(0, 2 * share), :] = small
        piece = back[:, step * cell : (step + 1) * cell]
        out[pl.ds(2 * share, share // 2), pl.ds(0, cell)] = piece[: share // 2]
        out[pl.ds(2 * share, share // 2), pl.ds(cell, cell)] = piece[share // 2 :]


def final_kernel(*refs, tiles, reps):
    own_corr, own_back, basis_ref = refs[:3]
    arrived = refs[3 : 2 + tiles]
    adj_out, corr_out, back = refs[2 + tiles :]
    share = own_back.shape[0]
    cell = own_back.shape[1]
    width2 = basis_ref.shape[3]
    width = width2 // 2
    block = basis_ref.shape[2]
    back[:, pl.ds(0, cell)] = own_back[...]
    corr = own_corr[...]
    for step in range(1, tiles):
        got = arrived[step - 1]
        corr = corr + got[pl.ds(0, 2 * share), :].astype(F32)
        back[pl.ds(0, share // 2), pl.ds(step * cell, cell)] = got[pl.ds(2 * share, share // 2), pl.ds(0, cell)]
        back[pl.ds(share // 2, share // 2), pl.ds(step * cell, cell)] = got[pl.ds(2 * share, share // 2), pl.ds(cell, cell)]
    image = dot(back[...], basis_ref[...].reshape(tiles * reps * block, width2), NN)
    adj_out[0] = image[:, :width]
    adj_out[1] = image[:, width:]
    corr_out[0] = corr[:share]
    corr_out[1] = corr[share:]


def call(kernel, ins, outs, scratch, args):
    vmem, smem = pl.BlockSpec(memory_space=pltpu.VMEM), pl.BlockSpec(memory_space=pltpu.SMEM)
    args = [pltpu.with_memory_space_constraint(a, pltpu.VMEM) if k == "p" else a for k, a in zip(ins, args)]
    return pl.pallas_call(
        kernel,
        in_specs=[smem if kind == "s" else vmem for kind in ins],
        out_specs=[vmem] * len(outs),
        out_shape=outs,
        scratch_shapes=scratch,
    )(*args)


def short_path(focusing, source, receiver, tile_ranks, keep_counts):
    tiles, reps = lax.axis_size("tile"), lax.axis_size("rep")
    ranks, width = source.shape[1], source.shape[3]
    points = focusing.shape[1]
    share = points // reps
    block = 2 * ranks
    factor = 1.0 / math.sqrt(SPAN * width * tiles)
    shaped, placed = jax.ShapeDtypeStruct, pltpu.VMEM
    order = sorted(range(1, tiles), reverse=True)
    rep_order = sorted(range(1, reps), key=lambda s: (s == 1, s))
    live = tile_ranks.reshape(tiles)

    made = call(
        forward_kernel,
        "svv",
        [placed((block, points), BF16)] * tiles,
        [pltpu.VMEM((tiles, block, points), BF16)],
        (live, source, focusing.reshape(2 * points, width)),
    )
    got = {step: swap(made[step], "tile", step) for step in order}
    lifts = {step: swap(receiver, "rep", step) for step in rep_order}
    gathered = jnp.concatenate([made[0]] + [got[step] for step in range(1, tiles)], axis=0)
    spread = {step: swap(gathered, "rep", step) for step in rep_order}
    bases = {step: swap(source, "rep", step) for step in rep_order}
    lift, weight = call(
        functools.partial(lift_kernel, reps=reps),
        "s" + "p" * reps,
        [placed((tiles, reps, block, 2 * width), BF16), placed((8, 2 * width), F32)],
        [],
        (keep_counts, receiver, *[lifts[step] for step in range(1, reps)]),
    )
    middle = call(
        functools.partial(middle_kernel, tiles=tiles, reps=reps, factor=factor),
        "p" * (reps + 2),
        [placed((2, share, width), F32), placed((2 * share, points), F32), placed((share, reps * block), BF16)]
        + [placed((2 * share + share // 2, points), BF16)] * (tiles - 1),
        [pltpu.VMEM((points, 2 * width), F32)],
        (gathered, *[spread[step] for step in range(1, reps)], lift, weight),
    )
    forward_data, own_corr, own_back = middle[:3]
    sent = {step: swap(middle[2 + step], "tile", step) for step in order}
    (basis,) = call(
        functools.partial(image_basis_kernel, reps=reps),
        "s" + "p" * reps,
        [placed((tiles, reps, block, 2 * width), BF16)],
        [],
        (live, source, *[bases[step] for step in range(1, reps)]),
    )
    adjoint, corr = call(
        functools.partial(final_kernel, tiles=tiles, reps=reps),
        "p" * (tiles + 2),
        [shaped((2, share, width), F32), shaped((2, share, points), F32)],
        [pltpu.VMEM((share, tiles * reps * block), BF16)],
        (own_corr, own_back, basis, *[sent[step] for step in range(1, tiles)]),
    )
    return forward_data, adjoint, corr


def bucket_live(rank_column, ranks):
    return (lax.iota(jnp.int32, ranks) // BUCKET)[:, None] < rank_column[None, :]


def long_path(focusing, source_basis, receiver_basis, tile_ranks, keep_counts):
    width = focusing.shape[2]
    share = focusing.shape[1] // lax.axis_size("rep")
    weights = (lax.iota(jnp.int32, width) < keep_counts[0]).astype(F32)
    factor = 1.0 / math.sqrt(SPAN * width * lax.axis_size("tile"))
    source = lax.all_gather(source_basis, "rep", axis=1, tiled=True)
    receiver = lax.all_gather(receiver_basis, "rep", axis=1, tiled=True)
    focal = lax.dynamic_slice_in_dim(focusing, lax.axis_index("rep") * share, share, 1)
    ranks, cells = source.shape[1], source.shape[2]
    live = bucket_live(tile_ranks[:, 0], ranks)

    blocks = dot(source.reshape(-1, width), focal.reshape(-1, width), NT)
    blocks = blocks.reshape(2, ranks, cells, 2, share)
    coef = jnp.stack([blocks[0, :, :, 0] - blocks[1, :, :, 1], blocks[0, :, :, 1] + blocks[1, :, :, 0]])
    coef = jnp.where(live[None, :, :, None], coef, 0.0).astype(BF16)[:, :, :, None]
    coef = lax.all_to_all(coef, "tile", split_axis=2, concat_axis=3, tiled=True)
    coef = coef.reshape(2, ranks * cells, share)
    flat = receiver.reshape(2, ranks * cells, width)
    blocks = jnp.einsum("wgh,lgj->wlhj", coef, flat, preferred_element_type=F32)
    forward_data = jnp.stack([blocks[0, 0] - blocks[1, 1], blocks[1, 0] + blocks[0, 1]])
    masked = (forward_data * weights).astype(BF16)

    blocks = jnp.einsum("pks,qfs->pqkf", flat, masked, preferred_element_type=F32)
    back = jnp.stack([blocks[0, 0] + blocks[1, 1], blocks[0, 1] - blocks[1, 0]]).astype(BF16)
    back = back.reshape(2, ranks, 1, cells, share)
    back = lax.all_to_all(back, "tile", split_axis=3, concat_axis=2, tiled=True)
    back = jnp.where(live[None, :, :, None, None], back, jnp.zeros((), BF16)).reshape(2, ranks * cells, share)
    flat = source.reshape(2, ranks * cells, width)
    blocks = jnp.einsum("wgh,lgj->wlhj", back, flat, preferred_element_type=F32)
    adjoint = jnp.stack([blocks[0, 0] + blocks[1, 1], blocks[1, 0] - blocks[0, 1]])
    blocks = jnp.einsum(
        "pgs,qfs->pqgf", adjoint, focusing.astype(F32), precision=lax.Precision.HIGHEST, preferred_element_type=F32
    )
    corr = factor * jnp.stack([blocks[0, 0] + blocks[1, 1], blocks[1, 0] - blocks[0, 1]])
    return forward_data, adjoint, lax.psum(corr, "tile")


def power_of_two(n):
    return n & (n - 1) == 0


def solution(mesh):
    tiles, reps = mesh.shape["tile"], mesh.shape["rep"]
    short = tiles <= 4 and power_of_two(tiles) and power_of_two(reps)

    def per_device(*args):
        return (short_path if short else long_path)(*args)

    placed = (
        P(None, "grp", "tile"),
        P(None, "rep", "grp", "tile"),
        P(None, "rep", "grp", "tile"),
        P("grp", "tile"),
        P(("grp", "tile")),
    )
    return jax.shard_map(
        per_device,
        mesh=mesh,
        in_specs=placed,
        out_specs=(P(None, ("grp", "rep"), "tile"), P(None, ("grp", "rep"), "tile"), P(None, "rep", "grp")),
        check_vma=False,
    )
```

```python
import functools
import math

import jax
import jax.numpy as jnp
from jax import lax
from jax.experimental import pallas as pl
from jax.experimental.pallas import tpu as pltpu
from jax.sharding import PartitionSpec as P


SPAN = 256
BUCKET = 16
BF16 = jnp.bfloat16
F32 = jnp.float32

NT = (((1,), (1,)), ((), ()))
NN = (((1,), (0,)), ((), ()))
TN = (((0,), (0,)), ((), ()))


def dot(a, b, dims):
    return lax.dot_general(a, b, dims, preferred_element_type=F32)


def swap(x, step):
    count = lax.axis_size("rep")
    return lax.ppermute(x, "rep", [(i, i ^ step) for i in range(count)])


def cross(x, step, twist=0):
    reps = lax.axis_size("rep")
    count = lax.axis_size("tile") * reps
    pairs = [(i, i ^ (step * reps) ^ (twist if i % 2 else 0)) for i in range(count)]
    return lax.ppermute(x, ("tile", "rep"), pairs)


LANES = 128


def live_rows(ranks_ref, cell, shard, ranks):
    rows = lax.broadcasted_iota(jnp.int32, (ranks, 1), 0) + shard * ranks
    return rows < ranks_ref[pl.ds(cell, 1), pl.ds(0, 1)] * BUCKET


def fetch_kernel(ranks_in, keep_in, *refs):
    count = (len(refs) - 4) // 2
    arrays, live_out, outs = refs[:count], refs[count], refs[count + 1 : 2 * count + 1]
    ranks_ref, keep_ref, sems = refs[2 * count + 1 :]
    scalars = [
        pltpu.make_async_copy(ranks_in, ranks_ref, sems.at[count]),
        pltpu.make_async_copy(keep_in, keep_ref, sems.at[count + 1]),
    ]
    copies = [pltpu.make_async_copy(ref, out, sems.at[i]) for i, (ref, out) in enumerate(zip(arrays, outs))]
    for copy in scalars + copies:
        copy.start()
    for copy in scalars:
        copy.wait()
    tiles = ranks_in.shape[0]
    for cell in range(tiles):
        live_out[pl.ds(cell, 1), :] = jnp.full((1, LANES), ranks_ref[cell], jnp.int32)
    live_out[pl.ds(tiles, 1), :] = jnp.full((1, LANES), keep_ref[0], jnp.int32)
    for copy in copies:
        copy.wait()


def forward_kernel(ranks_ref, own_ref, pair_ref, lift_ref, foc_ref, *refs):
    ranks, tiles = own_ref.shape[1], own_ref.shape[2]
    outs, bundle, blocks = refs[:tiles], refs[tiles], refs[tiles + 1]
    here = lax.axis_index("tile")
    me = lax.axis_index("rep")
    core = lax.rem(me, 2)
    points = foc_ref.shape[0] // 2
    pieces = (own_ref, pair_ref)
    rows = [ref[part, :, cell, :] for cell in range(tiles) for ref in pieces for part in range(2)]
    prod = dot(jnp.concatenate(rows, axis=0), foc_ref[...], NT)
    for cell in range(tiles):
        for shard in range(2):
            mask = live_rows(ranks_ref, cell, me ^ shard, ranks)
            first = (cell * 2 + shard) * 2 * ranks
            real = prod[first : first + ranks]
            imag = prod[first + ranks : first + 2 * ranks]
            coef = [real[:, :points] - imag[:, points:], real[:, points:] + imag[:, :points]]
            for part in range(2):
                spot = pl.multiple_of(((core ^ shard) * 2 + part) * ranks, ranks)
                blocks[cell, pl.ds(spot, ranks), :] = jnp.where(mask, coef[part], 0.0).astype(BF16)
    for step in range(tiles):
        outs[step][...] = blocks[here ^ step]
    size = 2 * ranks
    bundle[pl.ds(0, size)] = lift_ref[...].reshape(size, tiles, points)
    bundle[pl.ds(size, size)] = own_ref[...].reshape(size, tiles, points)
    own = blocks[here, pl.ds(pl.multiple_of(core * size, size), size), :]
    bundle[pl.ds(2 * size, size // tiles)] = own.reshape(size // tiles, tiles, points)


def put_lift(out, spot, slot, real, imag):
    ranks, width = real.shape
    out[spot, slot, pl.ds(0, ranks), pl.ds(0, width)] = real
    out[spot, slot, pl.ds(0, ranks), pl.ds(width, width)] = imag
    out[spot, slot, pl.ds(ranks, ranks), pl.ds(0, width)] = -imag
    out[spot, slot, pl.ds(ranks, ranks), pl.ds(width, width)] = real


def lift_kernel(live_ref, own_ref, pair_ref, far_ref, out, weight):
    ranks, tiles, width = own_ref.shape[1:]
    here = lax.axis_index("tile")
    core = lax.rem(lax.axis_index("rep"), 2)
    columns = lax.broadcasted_iota(jnp.int32, weight.shape, 1)
    columns = jnp.where(columns >= width, columns - width, columns)
    weight[...] = (columns < live_ref[pl.ds(tiles, 1), pl.ds(0, 1)]).astype(F32)
    for cell in range(tiles):
        spot = here ^ cell
        put_lift(out, spot, core, own_ref[0, :, cell, :], own_ref[1, :, cell, :])
        put_lift(out, spot, 1 - core, pair_ref[0, :, cell, :], pair_ref[1, :, cell, :])
        put_lift(out, spot, 2 + core, far_ref[pl.ds(0, ranks), cell, :], far_ref[pl.ds(ranks, ranks), cell, :])


def image_basis_kernel(ranks_ref, own_ref, pair_ref, far_ref, last_ref, out):
    ranks, tiles, width = own_ref.shape[1:]
    size = 2 * ranks
    here = lax.axis_index("tile")
    me = lax.axis_index("rep")
    core = lax.rem(me, 2)
    for cell in range(tiles):
        pieces = [(core, me, own_ref[0, :, cell, :], own_ref[1, :, cell, :])]
        pieces.append((1 - core, me ^ 1, pair_ref[0, :, cell, :], pair_ref[1, :, cell, :]))
        for slot, shard, ref in ((2 + core, me ^ 2, far_ref), (3 - core, me ^ 3, last_ref)):
            parts = [ref[pl.ds(size + part * ranks, ranks), cell, :] for part in range(2)]
            pieces.append((slot, shard, *parts))
        spot = here ^ cell
        for slot, shard, real, imag in pieces:
            mask = live_rows(ranks_ref, cell, shard, ranks)
            real = jnp.where(mask, real.astype(F32), 0.0)
            imag = jnp.where(mask, imag.astype(F32), 0.0)
            out[spot, slot, pl.ds(0, ranks), pl.ds(0, width)] = real.astype(BF16)
            out[spot, slot, pl.ds(0, ranks), pl.ds(width, width)] = (-imag).astype(BF16)
            out[spot, slot, pl.ds(ranks, ranks), pl.ds(0, width)] = imag.astype(BF16)
            out[spot, slot, pl.ds(ranks, ranks), pl.ds(width, width)] = real.astype(BF16)


def middle_kernel(near_ref, far_ref, last_ref, mine_ref, pair_ref, lift_in, weight_ref, *refs, factor):
    lift_ref, fwd_out, own_corr, own_back = refs[:4]
    tiles, reps, block, width2 = lift_ref.shape
    sends, whole, coef = refs[4 : 3 + tiles], refs[3 + tiles], refs[4 + tiles]
    me = lax.axis_index("rep")
    core = lax.rem(me, 2)
    here = lax.axis_index("tile")
    points = whole.shape[0]
    width = width2 // 2
    share = points // reps
    ranks = block // 2
    for cell in range(tiles):
        put_lift(
            lift_ref, here ^ cell, 3 - core, last_ref[pl.ds(0, ranks), cell, :], last_ref[pl.ds(ranks, ranks), cell, :]
        )
    coef[0, pl.ds(0, 2)] = near_ref[...].reshape(2, block, points)
    coef[0, 2 + core] = far_ref[pl.ds(2 * block, block // tiles)].reshape(block, points)
    coef[0, 3 - core] = last_ref[pl.ds(2 * block, block // tiles)].reshape(block, points)
    coef[pl.ds(1, tiles - 1), pl.ds(2 * core, 2)] = mine_ref[...].reshape(tiles - 1, 2, block, points)
    coef[pl.ds(1, tiles - 1), pl.ds(2 - 2 * core, 2)] = pair_ref[...].reshape(tiles - 1, 2, block, points)
    rows = tiles * reps * block
    total = dot(coef[...].reshape(rows, points), lift_ref[...].reshape(rows, width2), TN)
    whole[...] = total
    mine = whole[pl.ds(pl.multiple_of(me * share, share), share), :]
    fwd_out[0] = mine[:, :width]
    fwd_out[1] = mine[:, width:]
    muted = (mine * weight_ref[pl.ds(0, 1), :]).astype(BF16)
    back = dot(muted, lift_ref[...].reshape(tiles * reps * block, width2), NT).astype(BF16)
    cell = reps * block
    high = total.astype(BF16)
    low = (total - high.astype(F32)).astype(BF16)
    turned = jnp.concatenate([muted[:, width:], -muted[:, :width]], axis=1)
    left = jnp.concatenate([muted, turned], axis=0)
    corr = (dot(left, high, NT) + dot(left, low, NT)) * factor
    own_corr[...] = corr
    own_back[...] = back[:, :cell]
    small = corr.astype(BF16)
    for step in range(1, tiles):
        out = sends[step - 1]
        out[pl.ds(0, 2 * share), :] = small
        piece = back[:, step * cell : (step + 1) * cell]
        out[pl.ds(2 * share, share // 2), pl.ds(0, cell)] = piece[: share // 2]
        out[pl.ds(2 * share, share // 2), pl.ds(cell, cell)] = piece[share // 2 :]


def final_kernel(*refs, tiles, reps):
    own_corr, own_back, basis_ref = refs[:3]
    arrived = refs[3 : 2 + tiles]
    adj_out, corr_out, back = refs[2 + tiles :]
    share = own_back.shape[0]
    cell = own_back.shape[1]
    width2 = basis_ref.shape[3]
    width = width2 // 2
    block = basis_ref.shape[2]
    back[:, pl.ds(0, cell)] = own_back[...]
    corr = own_corr[...]
    for step in range(1, tiles):
        got = arrived[step - 1]
        corr = corr + got[pl.ds(0, 2 * share), :].astype(F32)
        back[pl.ds(0, share // 2), pl.ds(step * cell, cell)] = got[pl.ds(2 * share, share // 2), pl.ds(0, cell)]
        back[pl.ds(share // 2, share // 2), pl.ds(step * cell, cell)] = got[pl.ds(2 * share, share // 2), pl.ds(cell, cell)]
    image = dot(back[...], basis_ref[...].reshape(tiles * reps * block, width2), NN)
    adj_out[0] = image[:, :width]
    adj_out[1] = image[:, width:]
    corr_out[0] = corr[:share]
    corr_out[1] = corr[share:]


def call(kernel, ins, outs, scratch, args, aliases={}):
    vmem, smem = pl.BlockSpec(memory_space=pltpu.VMEM), pl.BlockSpec(memory_space=pltpu.SMEM)
    kinds = {"s": smem, "h": pl.BlockSpec(memory_space=pl.ANY), "p": vmem}
    args = [pltpu.with_memory_space_constraint(a, pltpu.VMEM) if k == "p" else a for k, a in zip(ins, args)]
    return pl.pallas_call(
        kernel,
        in_specs=[kinds[kind] for kind in ins],
        out_specs=[vmem] * len(outs),
        out_shape=outs,
        scratch_shapes=scratch,
        input_output_aliases=aliases,
    )(*args)


def short_path(focusing, source, receiver, tile_ranks, keep_counts):
    tiles, reps = lax.axis_size("tile"), lax.axis_size("rep")
    ranks, width = source.shape[1], source.shape[3]
    points = focusing.shape[1]
    share = points // reps
    block = 2 * ranks
    factor = 1.0 / math.sqrt(SPAN * width * tiles)
    shaped, placed = jax.ShapeDtypeStruct, pltpu.VMEM
    order = sorted(range(1, tiles), reverse=True)

    source_pair = swap(source, 1)
    live, source, receiver, foc = call(
        fetch_kernel,
        "hhhhh",
        [
            placed((8, LANES), jnp.int32),
            placed(source.shape, BF16),
            placed(receiver.shape, BF16),
            placed((2 * points, width), BF16),
        ],
        [pltpu.SMEM((tiles,), jnp.int32), pltpu.SMEM((1,), jnp.int32), pltpu.SemaphoreType.DMA((5,))],
        (tile_ranks.reshape(tiles), keep_counts, source, receiver, focusing.reshape(2 * points, width)),
    )
    made = call(
        forward_kernel,
        "ppppp",
        [placed((2 * block, points), BF16)] * tiles + [placed((2 * block + block // tiles, tiles, points), BF16)],
        [pltpu.VMEM((tiles, 2 * block, points), BF16)],
        (live, source, source_pair, receiver, foc),
    )
    far = swap(made[tiles], 2)
    got = {step: cross(made[step], step, 2) for step in order}
    receiver_pair = swap(receiver, 1)
    last = swap(far, 1)
    gathered = jnp.concatenate([got[step] for step in range(1, tiles)], axis=0)
    spread = swap(gathered, 1)
    lift, weight = call(
        lift_kernel,
        "pppp",
        [placed((tiles, reps, block, 2 * width), BF16), placed((8, 2 * width), F32)],
        [],
        (live, receiver, receiver_pair, far),
    )
    middle = call(
        functools.partial(middle_kernel, factor=factor),
        "ppppppp",
        [placed(lift.shape, BF16), placed((2, share, width), F32), placed((2 * share, points), F32), placed((share, reps * block), BF16)]
        + [placed((2 * share + share // 2, points), BF16)] * (tiles - 1),
        [pltpu.VMEM((points, 2 * width), F32), pltpu.VMEM((tiles, reps, block, points), BF16)],
        (made[0], far, last, gathered, spread, lift, weight),
        {5: 0},
    )
    forward_data, own_corr, own_back = middle[1:4]
    sent = {step: cross(middle[3 + step], step) for step in order}
    (basis,) = call(
        image_basis_kernel,
        "ppppp",
        [placed((tiles, reps, block, 2 * width), BF16)],
        [],
        (live, source, source_pair, far, last),
    )
    adjoint, corr = call(
        functools.partial(final_kernel, tiles=tiles, reps=reps),
        "p" * (tiles + 2),
        [shaped((2, share, width), F32), shaped((2, share, points), F32)],
        [pltpu.VMEM((share, tiles * reps * block), BF16)],
        (own_corr, own_back, basis, *[sent[step] for step in range(1, tiles)]),
    )
    return forward_data, adjoint, corr


def bucket_live(rank_column, ranks):
    return (lax.iota(jnp.int32, ranks) // BUCKET)[:, None] < rank_column[None, :]


def long_path(focusing, source_basis, receiver_basis, tile_ranks, keep_counts):
    width = focusing.shape[2]
    share = focusing.shape[1] // lax.axis_size("rep")
    weights = (lax.iota(jnp.int32, width) < keep_counts[0]).astype(F32)
    factor = 1.0 / math.sqrt(SPAN * width * lax.axis_size("tile"))
    source = lax.all_gather(source_basis, "rep", axis=1, tiled=True)
    receiver = lax.all_gather(receiver_basis, "rep", axis=1, tiled=True)
    focal = lax.dynamic_slice_in_dim(focusing, lax.axis_index("rep") * share, share, 1)
    ranks, cells = source.shape[1], source.shape[2]
    live = bucket_live(tile_ranks[:, 0], ranks)

    blocks = dot(source.reshape(-1, width), focal.reshape(-1, width), NT)
    blocks = blocks.reshape(2, ranks, cells, 2, share)
    coef = jnp.stack([blocks[0, :, :, 0] - blocks[1, :, :, 1], blocks[0, :, :, 1] + blocks[1, :, :, 0]])
    coef = jnp.where(live[None, :, :, None], coef, 0.0).astype(BF16)[:, :, :, None]
    coef = lax.all_to_all(coef, "tile", split_axis=2, concat_axis=3, tiled=True)
    coef = coef.reshape(2, ranks * cells, share)
    flat = receiver.reshape(2, ranks * cells, width)
    blocks = jnp.einsum("wgh,lgj->wlhj", coef, flat, preferred_element_type=F32)
    forward_data = jnp.stack([blocks[0, 0] - blocks[1, 1], blocks[1, 0] + blocks[0, 1]])
    masked = (forward_data * weights).astype(BF16)

    blocks = jnp.einsum("pks,qfs->pqkf", flat, masked, preferred_element_type=F32)
    back = jnp.stack([blocks[0, 0] + blocks[1, 1], blocks[0, 1] - blocks[1, 0]]).astype(BF16)
    back = back.reshape(2, ranks, 1, cells, share)
    back = lax.all_to_all(back, "tile", split_axis=3, concat_axis=2, tiled=True)
    back = jnp.where(live[None, :, :, None, None], back, jnp.zeros((), BF16)).reshape(2, ranks * cells, share)
    flat = source.reshape(2, ranks * cells, width)
    blocks = jnp.einsum("wgh,lgj->wlhj", back, flat, preferred_element_type=F32)
    adjoint = jnp.stack([blocks[0, 0] + blocks[1, 1], blocks[1, 0] - blocks[0, 1]])
    blocks = jnp.einsum(
        "pgs,qfs->pqgf", adjoint, focusing.astype(F32), precision=lax.Precision.HIGHEST, preferred_element_type=F32
    )
    corr = factor * jnp.stack([blocks[0, 0] + blocks[1, 1], blocks[1, 0] - blocks[0, 1]])
    return forward_data, adjoint, lax.psum(corr, "tile")


def solution(mesh):
    tiles, reps = mesh.shape["tile"], mesh.shape["rep"]
    short = tiles == 4 and reps == 4

    def per_device(*args):
        return (short_path if short else long_path)(*args)

    placed = (
        P(None, "grp", "tile"),
        P(None, "rep", "grp", "tile"),
        P(None, "rep", "grp", "tile"),
        P("grp", "tile"),
        P(("grp", "tile")),
    )
    return jax.shard_map(
        per_device,
        mesh=mesh,
        in_specs=placed,
        out_specs=(P(None, ("grp", "rep"), "tile"), P(None, ("grp", "rep"), "tile"), P(None, "rep", "grp")),
        check_vma=False,
    )
```

```python
import functools
import math

import jax
import jax.numpy as jnp
from jax import lax
from jax.experimental import pallas as pl
from jax.experimental.pallas import tpu as pltpu
from jax.sharding import PartitionSpec as P


SPAN = 256
BUCKET = 16
BF16 = jnp.bfloat16
F32 = jnp.float32

NT = (((1,), (1,)), ((), ()))
NN = (((1,), (0,)), ((), ()))
TN = (((0,), (0,)), ((), ()))


def dot(a, b, dims):
    return lax.dot_general(a, b, dims, preferred_element_type=F32)


def swap(x, step):
    count = lax.axis_size("rep")
    return lax.ppermute(x, "rep", [(i, i ^ step) for i in range(count)])


def cross(x, step, twist=0):
    reps = lax.axis_size("rep")
    count = lax.axis_size("tile") * reps
    pairs = [(i, i ^ (step * reps) ^ (twist if i % 2 else 0)) for i in range(count)]
    return lax.ppermute(x, ("tile", "rep"), pairs)


LANES = 128


def live_rows(ranks_ref, cell, shard, ranks):
    rows = lax.broadcasted_iota(jnp.int32, (ranks, 1), 0) + shard * ranks
    return rows < ranks_ref[pl.ds(cell, 1), pl.ds(0, 1)] * BUCKET


def fetch_kernel(ranks_in, *refs):
    count = (len(refs) - 3) // 2
    arrays, live_out, outs = refs[:count], refs[count], refs[count + 1 : 2 * count + 1]
    ranks_ref, sems = refs[2 * count + 1 :]
    scalars = pltpu.make_async_copy(ranks_in, ranks_ref, sems.at[count])
    copies = [pltpu.make_async_copy(ref, out, sems.at[i]) for i, (ref, out) in enumerate(zip(arrays, outs))]
    scalars.start()
    for copy in copies:
        copy.start()
    scalars.wait()
    for cell in range(ranks_in.shape[0]):
        live_out[pl.ds(cell, 1), :] = jnp.full((1, LANES), ranks_ref[cell], jnp.int32)
    for copy in copies:
        copy.wait()


def forward_kernel(ranks_ref, own_ref, pair_ref, lift_ref, foc_ref, *refs):
    ranks, tiles = own_ref.shape[1], own_ref.shape[2]
    outs, bundle, blocks = refs[:tiles], refs[tiles], refs[tiles + 1]
    here = lax.axis_index("tile")
    me = lax.axis_index("rep")
    core = lax.rem(me, 2)
    points = foc_ref.shape[0] // 2
    pieces = (own_ref, pair_ref)
    rows = [ref[part, :, cell, :] for cell in range(tiles) for ref in pieces for part in range(2)]
    prod = dot(jnp.concatenate(rows, axis=0), foc_ref[...], NT)
    for cell in range(tiles):
        for shard in range(2):
            mask = live_rows(ranks_ref, cell, me ^ shard, ranks)
            first = (cell * 2 + shard) * 2 * ranks
            real = prod[first : first + ranks]
            imag = prod[first + ranks : first + 2 * ranks]
            coef = [real[:, :points] - imag[:, points:], real[:, points:] + imag[:, :points]]
            for part in range(2):
                spot = pl.multiple_of(((core ^ shard) * 2 + part) * ranks, ranks)
                blocks[cell, pl.ds(spot, ranks), :] = jnp.where(mask, coef[part], 0.0).astype(BF16)
    for step in range(tiles):
        outs[step][...] = blocks[here ^ step]
    size = 2 * ranks
    bundle[pl.ds(0, size)] = lift_ref[...].reshape(size, tiles, points)
    bundle[pl.ds(size, size)] = own_ref[...].reshape(size, tiles, points)
    own = blocks[here, pl.ds(pl.multiple_of(core * size, size), size), :]
    bundle[pl.ds(2 * size, size // tiles)] = own.reshape(size // tiles, tiles, points)


def put_lift(out, spot, slot, real, imag):
    ranks, width = real.shape
    out[spot, slot, pl.ds(0, ranks), pl.ds(0, width)] = real
    out[spot, slot, pl.ds(0, ranks), pl.ds(width, width)] = imag
    out[spot, slot, pl.ds(ranks, ranks), pl.ds(0, width)] = -imag
    out[spot, slot, pl.ds(ranks, ranks), pl.ds(width, width)] = real


def lift_kernel(keep_ref, own_ref, pair_ref, far_ref, out, weight):
    ranks, tiles, width = own_ref.shape[1:]
    columns = lax.broadcasted_iota(jnp.int32, weight.shape, 1)
    columns = jnp.where(columns >= width, columns - width, columns)
    weight[...] = (columns < keep_ref[0]).astype(F32)
    here = lax.axis_index("tile")
    core = lax.rem(lax.axis_index("rep"), 2)
    for cell in range(tiles):
        spot = here ^ cell
        put_lift(out, spot, core, own_ref[0, :, cell, :], own_ref[1, :, cell, :])
        put_lift(out, spot, 1 - core, pair_ref[0, :, cell, :], pair_ref[1, :, cell, :])
        put_lift(out, spot, 2 + core, far_ref[pl.ds(0, ranks), cell, :], far_ref[pl.ds(ranks, ranks), cell, :])


def image_basis_kernel(ranks_ref, own_ref, pair_ref, far_ref, last_ref, out):
    ranks, tiles, width = own_ref.shape[1:]
    size = 2 * ranks
    here = lax.axis_index("tile")
    me = lax.axis_index("rep")
    core = lax.rem(me, 2)
    for cell in range(tiles):
        pieces = [(core, me, own_ref[0, :, cell, :], own_ref[1, :, cell, :])]
        pieces.append((1 - core, me ^ 1, pair_ref[0, :, cell, :], pair_ref[1, :, cell, :]))
        for slot, shard, ref in ((2 + core, me ^ 2, far_ref), (3 - core, me ^ 3, last_ref)):
            parts = [ref[pl.ds(size + part * ranks, ranks), cell, :] for part in range(2)]
            pieces.append((slot, shard, *parts))
        spot = here ^ cell
        for slot, shard, real, imag in pieces:
            mask = live_rows(ranks_ref, cell, shard, ranks)
            real = jnp.where(mask, real.astype(F32), 0.0)
            imag = jnp.where(mask, imag.astype(F32), 0.0)
            out[spot, slot, pl.ds(0, ranks), pl.ds(0, width)] = real.astype(BF16)
            out[spot, slot, pl.ds(0, ranks), pl.ds(width, width)] = (-imag).astype(BF16)
            out[spot, slot, pl.ds(ranks, ranks), pl.ds(0, width)] = imag.astype(BF16)
            out[spot, slot, pl.ds(ranks, ranks), pl.ds(width, width)] = real.astype(BF16)


def early_kernel(near_ref, far_ref, last_ref, mine_ref, lift_in, lift_ref, part_out, coef):
    tiles, reps, block, width2 = lift_ref.shape
    core = lax.rem(lax.axis_index("rep"), 2)
    here = lax.axis_index("tile")
    points = part_out.shape[0]
    ranks = block // 2
    for cell in range(tiles):
        put_lift(
            lift_ref, here ^ cell, 3 - core, last_ref[pl.ds(0, ranks), cell, :], last_ref[pl.ds(ranks, ranks), cell, :]
        )
    coef[pl.ds(0, 2)] = near_ref[...].reshape(2, block, points)
    coef[2 + core] = far_ref[pl.ds(2 * block, block // tiles)].reshape(block, points)
    coef[3 - core] = last_ref[pl.ds(2 * block, block // tiles)].reshape(block, points)
    rows = (tiles - 1) * 2 * block
    part = dot(coef[...].reshape(reps * block, points), lift_ref[0].reshape(reps * block, width2), TN)
    lift = lift_ref[pl.ds(1, tiles - 1), pl.ds(2 * core, 2)].reshape(rows, width2)
    part_out[...] = part + dot(mine_ref[...], lift, TN)


def middle_kernel(weight_ref, pair_ref, lift_ref, part_ref, *refs, factor):
    fwd_out, own_corr, own_back = refs[:3]
    tiles, reps, block, width2 = lift_ref.shape
    sends, whole = refs[3 : 2 + tiles], refs[2 + tiles]
    me = lax.axis_index("rep")
    core = lax.rem(me, 2)
    points = whole.shape[0]
    width = width2 // 2
    share = points // reps
    lift = lift_ref[pl.ds(1, tiles - 1), pl.ds(2 - 2 * core, 2)].reshape((tiles - 1) * 2 * block, width2)
    total = part_ref[...] + dot(pair_ref[...], lift, TN)
    whole[...] = total
    mine = whole[pl.ds(pl.multiple_of(me * share, share), share), :]
    fwd_out[0] = mine[:, :width]
    fwd_out[1] = mine[:, width:]
    muted = (mine * weight_ref[pl.ds(0, 1), :]).astype(BF16)
    back = dot(muted, lift_ref[...].reshape(tiles * reps * block, width2), NT).astype(BF16)
    cell = reps * block
    high = total.astype(BF16)
    low = (total - high.astype(F32)).astype(BF16)
    turned = jnp.concatenate([muted[:, width:], -muted[:, :width]], axis=1)
    left = jnp.concatenate([muted, turned], axis=0)
    corr = (dot(left, high, NT) + dot(left, low, NT)) * factor
    own_corr[...] = corr
    own_back[...] = back[:, :cell]
    small = corr.astype(BF16)
    for step in range(1, tiles):
        out = sends[step - 1]
        out[pl.ds(0, 2 * share), :] = small
        piece = back[:, step * cell : (step + 1) * cell]
        out[pl.ds(2 * share, share // 2), pl.ds(0, cell)] = piece[: share // 2]
        out[pl.ds(2 * share, share // 2), pl.ds(cell, cell)] = piece[share // 2 :]


def final_kernel(own_corr, own_back, basis_ref, *refs):
    tiles, reps, block, width2 = basis_ref.shape
    arrived = refs[: tiles - 1]
    adj_out, corr_out, adj, corr, back, sems = refs[tiles - 1 :]
    share, cell = own_back.shape
    width = width2 // 2
    half = share // 2
    for part in range(2):
        rows = pl.ds(part * share, share)
        total = own_corr[rows, :]
        for got in arrived:
            total = total + got[rows, :].astype(F32)
        corr[part] = total
    first = pltpu.make_async_copy(corr, corr_out, sems.at[0])
    first.start()
    back[:, pl.ds(0, cell)] = own_back[...]
    for step, got in enumerate(arrived, 1):
        for part in range(2):
            back[pl.ds(part * half, half), pl.ds(step * cell, cell)] = got[
                pl.ds(2 * share, half), pl.ds(part * cell, cell)
            ]
    image = dot(back[...], basis_ref[...].reshape(tiles * reps * block, width2), NN)
    adj[0] = image[:, :width]
    adj[1] = image[:, width:]
    second = pltpu.make_async_copy(adj, adj_out, sems.at[1])
    second.start()
    first.wait()
    second.wait()


def call(kernel, ins, outs, scratch, args, aliases={}):
    vmem, smem = pl.BlockSpec(memory_space=pltpu.VMEM), pl.BlockSpec(memory_space=pltpu.SMEM)
    kinds = {"s": smem, "h": pl.BlockSpec(memory_space=pl.ANY), "p": vmem}
    args = [pltpu.with_memory_space_constraint(a, pltpu.VMEM) if k == "p" else a for k, a in zip(ins, args)]
    return pl.pallas_call(
        kernel,
        in_specs=[kinds[kind] for kind in ins],
        out_specs=[vmem if isinstance(out, pl.MemoryRef) else kinds["h"] for out in outs],
        out_shape=outs,
        scratch_shapes=scratch,
        input_output_aliases=aliases,
    )(*args)


def short_path(focusing, source, receiver, tile_ranks, keep_counts):
    tiles, reps = lax.axis_size("tile"), lax.axis_size("rep")
    ranks, width = source.shape[1], source.shape[3]
    points = focusing.shape[1]
    share = points // reps
    block = 2 * ranks
    factor = 1.0 / math.sqrt(SPAN * width * tiles)
    shaped, placed = jax.ShapeDtypeStruct, pltpu.VMEM
    order = sorted(range(1, tiles), reverse=True)

    source_pair = swap(source, 1)
    receiver_pair = swap(receiver, 1)
    live, source, receiver, foc = call(
        fetch_kernel,
        "hhhh",
        [
            placed((8, LANES), jnp.int32),
            placed(source.shape, BF16),
            placed(receiver.shape, BF16),
            placed((2 * points, width), BF16),
        ],
        [pltpu.SMEM((tiles,), jnp.int32), pltpu.SemaphoreType.DMA((4,))],
        (tile_ranks.reshape(tiles), source, receiver, focusing.reshape(2 * points, width)),
    )
    made = call(
        forward_kernel,
        "ppppp",
        [placed((2 * block, points), BF16)] * tiles + [placed((2 * block + block // tiles, tiles, points), BF16)],
        [pltpu.VMEM((tiles, 2 * block, points), BF16)],
        (live, source, source_pair, receiver, foc),
    )
    far = swap(made[tiles], 2)
    got = {step: cross(made[step], step, 2) for step in order}
    last = swap(far, 1)
    gathered = jnp.concatenate([got[step] for step in range(1, tiles)], axis=0)
    spread = swap(gathered, 1)
    lift, weight = call(
        lift_kernel,
        "sppp",
        [placed((tiles, reps, block, 2 * width), BF16), placed((8, 2 * width), F32)],
        [],
        (keep_counts, receiver, receiver_pair, far),
    )
    lift, part = call(
        early_kernel,
        "ppppp",
        [placed(lift.shape, BF16), placed((points, 2 * width), F32)],
        [pltpu.VMEM((reps, block, points), BF16)],
        (made[0], far, last, gathered, lift),
        {4: 0},
    )
    middle = call(
        functools.partial(middle_kernel, factor=factor),
        "pppp",
        [placed((2, share, width), F32), placed((2 * share, points), F32), placed((share, reps * block), BF16)]
        + [placed((2 * share + share // 2, points), BF16)] * (tiles - 1),
        [pltpu.VMEM((points, 2 * width), F32)],
        (weight, spread, lift, part),
    )
    forward_data, own_corr, own_back = middle[:3]
    sent = {step: cross(middle[2 + step], step) for step in order}
    (basis,) = call(
        image_basis_kernel,
        "ppppp",
        [placed((tiles, reps, block, 2 * width), BF16)],
        [],
        (live, source, source_pair, far, last),
    )
    adjoint, corr = call(
        final_kernel,
        "p" * (tiles + 2),
        [shaped((2, share, width), F32), shaped((2, share, points), F32)],
        [
            pltpu.VMEM((2, share, width), F32),
            pltpu.VMEM((2, share, points), F32),
            pltpu.VMEM((share, tiles * reps * block), BF16),
            pltpu.SemaphoreType.DMA((2,)),
        ],
        (own_corr, own_back, basis, *[sent[step] for step in range(1, tiles)]),
    )
    return forward_data, adjoint, corr


def bucket_live(rank_column, ranks):
    return (lax.iota(jnp.int32, ranks) // BUCKET)[:, None] < rank_column[None, :]


def long_path(focusing, source_basis, receiver_basis, tile_ranks, keep_counts):
    width = focusing.shape[2]
    share = focusing.shape[1] // lax.axis_size("rep")
    weights = (lax.iota(jnp.int32, width) < keep_counts[0]).astype(F32)
    factor = 1.0 / math.sqrt(SPAN * width * lax.axis_size("tile"))
    source = lax.all_gather(source_basis, "rep", axis=1, tiled=True)
    receiver = lax.all_gather(receiver_basis, "rep", axis=1, tiled=True)
    focal = lax.dynamic_slice_in_dim(focusing, lax.axis_index("rep") * share, share, 1)
    ranks, cells = source.shape[1], source.shape[2]
    live = bucket_live(tile_ranks[:, 0], ranks)

    blocks = dot(source.reshape(-1, width), focal.reshape(-1, width), NT)
    blocks = blocks.reshape(2, ranks, cells, 2, share)
    coef = jnp.stack([blocks[0, :, :, 0] - blocks[1, :, :, 1], blocks[0, :, :, 1] + blocks[1, :, :, 0]])
    coef = jnp.where(live[None, :, :, None], coef, 0.0).astype(BF16)[:, :, :, None]
    coef = lax.all_to_all(coef, "tile", split_axis=2, concat_axis=3, tiled=True)
    coef = coef.reshape(2, ranks * cells, share)
    flat = receiver.reshape(2, ranks * cells, width)
    blocks = jnp.einsum("wgh,lgj->wlhj", coef, flat, preferred_element_type=F32)
    forward_data = jnp.stack([blocks[0, 0] - blocks[1, 1], blocks[1, 0] + blocks[0, 1]])
    masked = (forward_data * weights).astype(BF16)

    blocks = jnp.einsum("pks,qfs->pqkf", flat, masked, preferred_element_type=F32)
    back = jnp.stack([blocks[0, 0] + blocks[1, 1], blocks[0, 1] - blocks[1, 0]]).astype(BF16)
    back = back.reshape(2, ranks, 1, cells, share)
    back = lax.all_to_all(back, "tile", split_axis=3, concat_axis=2, tiled=True)
    back = jnp.where(live[None, :, :, None, None], back, jnp.zeros((), BF16)).reshape(2, ranks * cells, share)
    flat = source.reshape(2, ranks * cells, width)
    blocks = jnp.einsum("wgh,lgj->wlhj", back, flat, preferred_element_type=F32)
    adjoint = jnp.stack([blocks[0, 0] + blocks[1, 1], blocks[1, 0] - blocks[0, 1]])
    blocks = jnp.einsum(
        "pgs,qfs->pqgf", adjoint, focusing.astype(F32), precision=lax.Precision.HIGHEST, preferred_element_type=F32
    )
    corr = factor * jnp.stack([blocks[0, 0] + blocks[1, 1], blocks[1, 0] - blocks[0, 1]])
    return forward_data, adjoint, lax.psum(corr, "tile")


def solution(mesh):
    tiles, reps = mesh.shape["tile"], mesh.shape["rep"]
    short = tiles == 4 and reps == 4

    def per_device(*args):
        return (short_path if short else long_path)(*args)

    placed = (
        P(None, "grp", "tile"),
        P(None, "rep", "grp", "tile"),
        P(None, "rep", "grp", "tile"),
        P("grp", "tile"),
        P(("grp", "tile")),
    )
    return jax.shard_map(
        per_device,
        mesh=mesh,
        in_specs=placed,
        out_specs=(P(None, ("grp", "rep"), "tile"), P(None, ("grp", "rep"), "tile"), P(None, "rep", "grp")),
        check_vma=False,
    )
```

```python
import functools
import math

import jax
import jax.numpy as jnp
from jax import lax
from jax.experimental import pallas as pl
from jax.experimental.pallas import tpu as pltpu
from jax.sharding import PartitionSpec as P


SPAN = 256
BUCKET = 16
BF16 = jnp.bfloat16
F32 = jnp.float32

NT = (((1,), (1,)), ((), ()))
NN = (((1,), (0,)), ((), ()))
TN = (((0,), (0,)), ((), ()))


def dot(a, b, dims):
    return lax.dot_general(a, b, dims, preferred_element_type=F32)


def swap(x, step):
    count = lax.axis_size("rep")
    return lax.ppermute(x, "rep", [(i, i ^ step) for i in range(count)])


def cross(x, step, twist=0):
    reps = lax.axis_size("rep")
    count = lax.axis_size("tile") * reps
    pairs = [(i, i ^ (step * reps) ^ (twist if i % 2 else 0)) for i in range(count)]
    return lax.ppermute(x, ("tile", "rep"), pairs)


LANES = 128


def live_rows(ranks_ref, cell, shard, ranks):
    rows = lax.broadcasted_iota(jnp.int32, (ranks, 1), 0) + shard * ranks
    return rows < ranks_ref[pl.ds(cell, 1), pl.ds(0, 1)] * BUCKET


def fetch_kernel(ranks_in, *refs):
    count = (len(refs) - 3) // 2
    arrays, live_out, outs = refs[:count], refs[count], refs[count + 1 : 2 * count + 1]
    ranks_ref, sems = refs[2 * count + 1 :]
    scalars = pltpu.make_async_copy(ranks_in, ranks_ref, sems.at[count])
    copies = [pltpu.make_async_copy(ref, out, sems.at[i]) for i, (ref, out) in enumerate(zip(arrays, outs))]
    scalars.start()
    for copy in copies:
        copy.start()
    scalars.wait()
    for cell in range(ranks_in.shape[0]):
        live_out[pl.ds(cell, 1), :] = jnp.full((1, LANES), ranks_ref[cell], jnp.int32)
    for copy in copies:
        copy.wait()


def forward_kernel(ranks_ref, own_ref, pair_ref, lift_ref, foc_ref, *refs):
    ranks, tiles = own_ref.shape[1], own_ref.shape[2]
    outs, bundle, blocks = refs[:tiles], refs[tiles], refs[tiles + 1]
    here = lax.axis_index("tile")
    me = lax.axis_index("rep")
    core = lax.rem(me, 2)
    points = foc_ref.shape[0] // 2
    pieces = (own_ref, pair_ref)
    rows = [ref[part, :, cell, :] for cell in range(tiles) for ref in pieces for part in range(2)]
    prod = dot(jnp.concatenate(rows, axis=0), foc_ref[...], NT)
    for cell in range(tiles):
        for shard in range(2):
            mask = live_rows(ranks_ref, cell, me ^ shard, ranks)
            first = (cell * 2 + shard) * 2 * ranks
            real = prod[first : first + ranks]
            imag = prod[first + ranks : first + 2 * ranks]
            coef = [real[:, :points] - imag[:, points:], real[:, points:] + imag[:, :points]]
            for part in range(2):
                spot = pl.multiple_of(((core ^ shard) * 2 + part) * ranks, ranks)
                blocks[cell, pl.ds(spot, ranks), :] = jnp.where(mask, coef[part], 0.0).astype(BF16)
    for step in range(tiles):
        outs[step][...] = blocks[here ^ step]
    size = 2 * ranks
    bundle[pl.ds(0, size)] = lift_ref[...].reshape(size, tiles, points)
    bundle[pl.ds(size, size)] = own_ref[...].reshape(size, tiles, points)
    own = blocks[here, pl.ds(pl.multiple_of(core * size, size), size), :]
    bundle[pl.ds(2 * size, size // tiles)] = own.reshape(size // tiles, tiles, points)


def put_lift(out, spot, slot, real, imag):
    ranks, width = real.shape
    out[spot, slot, pl.ds(0, ranks), pl.ds(0, width)] = real
    out[spot, slot, pl.ds(0, ranks), pl.ds(width, width)] = imag
    out[spot, slot, pl.ds(ranks, ranks), pl.ds(0, width)] = -imag
    out[spot, slot, pl.ds(ranks, ranks), pl.ds(width, width)] = real


def lift_kernel(keep_ref, own_ref, pair_ref, far_ref, out, weight):
    ranks, tiles, width = own_ref.shape[1:]
    columns = lax.broadcasted_iota(jnp.int32, weight.shape, 1)
    columns = jnp.where(columns >= width, columns - width, columns)
    weight[...] = (columns < keep_ref[0]).astype(F32)
    here = lax.axis_index("tile")
    core = lax.rem(lax.axis_index("rep"), 2)
    for cell in range(tiles):
        spot = here ^ cell
        put_lift(out, spot, core, own_ref[0, :, cell, :], own_ref[1, :, cell, :])
        put_lift(out, spot, 1 - core, pair_ref[0, :, cell, :], pair_ref[1, :, cell, :])
        put_lift(out, spot, 2 + core, far_ref[pl.ds(0, ranks), cell, :], far_ref[pl.ds(ranks, ranks), cell, :])


def image_basis_kernel(ranks_ref, own_ref, pair_ref, far_ref, last_ref, out):
    ranks, tiles, width = own_ref.shape[1:]
    size = 2 * ranks
    here = lax.axis_index("tile")
    me = lax.axis_index("rep")
    core = lax.rem(me, 2)
    for cell in range(tiles):
        pieces = [(core, me, own_ref[0, :, cell, :], own_ref[1, :, cell, :])]
        pieces.append((1 - core, me ^ 1, pair_ref[0, :, cell, :], pair_ref[1, :, cell, :]))
        for slot, shard, ref in ((2 + core, me ^ 2, far_ref), (3 - core, me ^ 3, last_ref)):
            parts = [ref[pl.ds(size + part * ranks, ranks), cell, :] for part in range(2)]
            pieces.append((slot, shard, *parts))
        spot = here ^ cell
        for slot, shard, real, imag in pieces:
            mask = live_rows(ranks_ref, cell, shard, ranks)
            real = jnp.where(mask, real.astype(F32), 0.0)
            imag = jnp.where(mask, imag.astype(F32), 0.0)
            out[spot, slot, pl.ds(0, ranks), pl.ds(0, width)] = real.astype(BF16)
            out[spot, slot, pl.ds(0, ranks), pl.ds(width, width)] = (-imag).astype(BF16)
            out[spot, slot, pl.ds(ranks, ranks), pl.ds(0, width)] = imag.astype(BF16)
            out[spot, slot, pl.ds(ranks, ranks), pl.ds(width, width)] = real.astype(BF16)


def early_kernel(near_ref, far_ref, last_ref, mine_ref, lift_in, lift_ref, part_out, coef):
    tiles, reps, block, width2 = lift_ref.shape
    core = lax.rem(lax.axis_index("rep"), 2)
    here = lax.axis_index("tile")
    points = part_out.shape[0]
    ranks = block // 2
    for cell in range(tiles):
        put_lift(
            lift_ref, here ^ cell, 3 - core, last_ref[pl.ds(0, ranks), cell, :], last_ref[pl.ds(ranks, ranks), cell, :]
        )
    coef[pl.ds(0, 2)] = near_ref[...].reshape(2, block, points)
    coef[2 + core] = far_ref[pl.ds(2 * block, block // tiles)].reshape(block, points)
    coef[3 - core] = last_ref[pl.ds(2 * block, block // tiles)].reshape(block, points)
    rows = (tiles - 1) * 2 * block
    part = dot(coef[...].reshape(reps * block, points), lift_ref[0].reshape(reps * block, width2), TN)
    lift = lift_ref[pl.ds(1, tiles - 1), pl.ds(2 * core, 2)].reshape(rows, width2)
    part_out[...] = part + dot(mine_ref[...], lift, TN)


def middle_kernel(weight_ref, pair_ref, lift_ref, part_ref, *refs, factor):
    fwd_out, own_corr, own_back = refs[:3]
    tiles, reps, block, width2 = lift_ref.shape
    sends, whole, high = refs[3 : 2 + tiles], refs[2 + tiles], refs[3 + tiles]
    me = lax.axis_index("rep")
    core = lax.rem(me, 2)
    points = whole.shape[0]
    width = width2 // 2
    share = points // reps
    lift = lift_ref[pl.ds(1, tiles - 1), pl.ds(2 - 2 * core, 2)].reshape((tiles - 1) * 2 * block, width2)
    total = part_ref[...] + dot(pair_ref[...], lift, TN)
    small = total.astype(BF16)
    whole[...] = total
    high[pl.ds(0, points), :] = small
    high[pl.ds(points, points), :] = small
    first = pl.multiple_of(me * share, share)
    mine = whole[pl.ds(first, share), :]
    fwd_out[0] = mine[:, :width]
    fwd_out[1] = mine[:, width:]
    muted = (mine * weight_ref[pl.ds(0, 1), :]).astype(BF16)
    back = dot(muted, lift_ref[...].reshape(tiles * reps * block, width2), NT).astype(BF16)
    cell = reps * block
    turned = jnp.concatenate([muted[:, width:], -muted[:, :width]], axis=1)
    left = jnp.concatenate([muted, turned], axis=0)
    corr = dot(left, high[pl.ds(first, points), :], NT) * factor
    own_corr[...] = corr
    own_back[...] = back[:, :cell]
    mixed = (corr[:share, :share] + corr[share:, :share]).astype(BF16)
    rest = corr.astype(BF16)
    group = share * (cell - share) // points
    for step in range(1, tiles):
        out = sends[step - 1]
        piece = back[:, step * cell : (step + 1) * cell]
        out[pl.ds(0, 2 * share), :] = rest
        out[pl.ds(0, share), pl.ds(0, share)] = mixed
        out[pl.ds(share, share), pl.ds(0, share)] = piece[:, :share]
        for part in range(share // group):
            rows = piece[part * group : (part + 1) * group, share:]
            out[pl.ds(2 * share, group), pl.ds(part * share, share)] = rows


def unpacked(got, out):
    share, cell = out.shape
    group = share * (cell - share) // got.shape[1]
    out[:, pl.ds(0, share)] = got[pl.ds(share, share), pl.ds(0, share)]
    for part in range(share // group):
        rows = got[pl.ds(2 * share, group), pl.ds(part * share, share)]
        out[pl.ds(part * group, group), pl.ds(share, cell - share)] = rows


def sum_kernel(own_back, basis_ref, *refs):
    tiles, _, _, width2 = basis_ref.shape
    arrived, (image_out, corr_out, back) = refs[: tiles - 2], refs[tiles - 2 :]
    share, cell = own_back.shape
    image = dot(own_back[...], basis_ref[0].reshape(cell, width2), NN)
    for step, got in enumerate(arrived, 1):
        unpacked(got, back)
        image += dot(back[...], basis_ref[step].reshape(cell, width2), NN)
    image_out[...] = image
    corr_out[...] = sum(got[pl.ds(0, 2 * share), :].astype(F32) for got in arrived)


def final_kernel(own_corr, corr_ref, image_ref, basis_ref, got, adj_out, corr_out, adj, corr, back, sems):
    tiles, _, _, width2 = basis_ref.shape
    share, cell = back.shape
    points = own_corr.shape[1]
    width = width2 // 2
    unpacked(got, back)
    image = image_ref[...] + dot(back[...], basis_ref[tiles - 1].reshape(cell, width2), NN)
    adj[0] = image[:, :width]
    adj[1] = image[:, width:]
    first = pltpu.make_async_copy(adj, adj_out, sems.at[0])
    first.start()
    arrived = corr_ref[...] + got[pl.ds(0, 2 * share), :].astype(F32)
    mixed = arrived[:share, :share] * 0.5
    turned = mixed.T
    shift = lax.axis_index("rep") * share
    lanes = lax.broadcasted_iota(jnp.int32, (share, points), 1)
    for part, block_sum in enumerate((mixed + turned, mixed - turned)):
        rows = slice(part * share, (part + 1) * share)
        padded = jnp.concatenate([block_sum, jnp.zeros((share, points - share), F32)], axis=1)
        total = own_corr[rows, :] + jnp.where(lanes < share, padded, arrived[rows])
        corr[part] = pltpu.roll(total, shift, 1)
    second = pltpu.make_async_copy(corr, corr_out, sems.at[1])
    second.start()
    first.wait()
    second.wait()


def call(kernel, ins, outs, scratch, args, aliases={}):
    vmem, smem = pl.BlockSpec(memory_space=pltpu.VMEM), pl.BlockSpec(memory_space=pltpu.SMEM)
    kinds = {"s": smem, "h": pl.BlockSpec(memory_space=pl.ANY), "p": vmem}
    args = [pltpu.with_memory_space_constraint(a, pltpu.VMEM) if k == "p" else a for k, a in zip(ins, args)]
    return pl.pallas_call(
        kernel,
        in_specs=[kinds[kind] for kind in ins],
        out_specs=[vmem if isinstance(out, pl.MemoryRef) else kinds["h"] for out in outs],
        out_shape=outs,
        scratch_shapes=scratch,
        input_output_aliases=aliases,
    )(*args)


def short_path(focusing, source, receiver, tile_ranks, keep_counts):
    tiles, reps = lax.axis_size("tile"), lax.axis_size("rep")
    ranks, width = source.shape[1], source.shape[3]
    points = focusing.shape[1]
    share = points // reps
    block = 2 * ranks
    factor = 1.0 / math.sqrt(SPAN * width * tiles)
    shaped, placed = jax.ShapeDtypeStruct, pltpu.VMEM
    order = sorted(range(1, tiles), reverse=True)

    source_pair = swap(source, 1)
    receiver_pair = swap(receiver, 1)
    live, source, receiver, foc = call(
        fetch_kernel,
        "hhhh",
        [
            placed((8, LANES), jnp.int32),
            placed(source.shape, BF16),
            placed(receiver.shape, BF16),
            placed((2 * points, width), BF16),
        ],
        [pltpu.SMEM((tiles,), jnp.int32), pltpu.SemaphoreType.DMA((4,))],
        (tile_ranks.reshape(tiles), source, receiver, focusing.reshape(2 * points, width)),
    )
    made = call(
        forward_kernel,
        "ppppp",
        [placed((2 * block, points), BF16)] * tiles + [placed((2 * block + block // tiles, tiles, points), BF16)],
        [pltpu.VMEM((tiles, 2 * block, points), BF16)],
        (live, source, source_pair, receiver, foc),
    )
    far = swap(made[tiles], 2)
    got = {step: cross(made[step], step, 2) for step in order}
    last = swap(far, 1)
    gathered = jnp.concatenate([got[step] for step in range(1, tiles)], axis=0)
    spread = swap(gathered, 1)
    lift, weight = call(
        lift_kernel,
        "sppp",
        [placed((tiles, reps, block, 2 * width), BF16), placed((8, 2 * width), F32)],
        [],
        (keep_counts, receiver, receiver_pair, far),
    )
    lift, part = call(
        early_kernel,
        "ppppp",
        [placed(lift.shape, BF16), placed((points, 2 * width), F32)],
        [pltpu.VMEM((reps, block, points), BF16)],
        (made[0], far, last, gathered, lift),
        {4: 0},
    )
    middle = call(
        functools.partial(middle_kernel, factor=factor),
        "pppp",
        [placed((2, share, width), F32), placed((2 * share, points), F32), placed((share, reps * block), BF16)]
        + [placed((2 * share + share * (reps * block - share) // points, points), BF16)] * (tiles - 1),
        [pltpu.VMEM((points, 2 * width), F32), pltpu.VMEM((2 * points, 2 * width), BF16)],
        (weight, spread, lift, part),
    )
    forward_data, own_corr, own_back = middle[:3]
    sent = {step: cross(middle[2 + step], step) for step in order}
    (basis,) = call(
        image_basis_kernel,
        "ppppp",
        [placed((tiles, reps, block, 2 * width), BF16)],
        [],
        (live, source, source_pair, far, last),
    )
    image_part, corr_part = call(
        sum_kernel,
        "p" * tiles,
        [placed((share, 2 * width), F32), placed((2 * share, points), F32)],
        [pltpu.VMEM((share, reps * block), BF16)],
        (own_back, basis, *[sent[step] for step in range(1, tiles - 1)]),
    )
    adjoint, corr = call(
        final_kernel,
        "ppppp",
        [shaped((2, share, width), F32), shaped((2, share, points), F32)],
        [
            pltpu.VMEM((2, share, width), F32),
            pltpu.VMEM((2, share, points), F32),
            pltpu.VMEM((share, reps * block), BF16),
            pltpu.SemaphoreType.DMA((2,)),
        ],
        (own_corr, corr_part, image_part, basis, sent[tiles - 1]),
    )
    return forward_data, adjoint, corr


def bucket_live(rank_column, ranks):
    return (lax.iota(jnp.int32, ranks) // BUCKET)[:, None] < rank_column[None, :]


def long_path(focusing, source_basis, receiver_basis, tile_ranks, keep_counts):
    width = focusing.shape[2]
    share = focusing.shape[1] // lax.axis_size("rep")
    weights = (lax.iota(jnp.int32, width) < keep_counts[0]).astype(F32)
    factor = 1.0 / math.sqrt(SPAN * width * lax.axis_size("tile"))
    source = lax.all_gather(source_basis, "rep", axis=1, tiled=True)
    receiver = lax.all_gather(receiver_basis, "rep", axis=1, tiled=True)
    focal = lax.dynamic_slice_in_dim(focusing, lax.axis_index("rep") * share, share, 1)
    ranks, cells = source.shape[1], source.shape[2]
    live = bucket_live(tile_ranks[:, 0], ranks)

    blocks = dot(source.reshape(-1, width), focal.reshape(-1, width), NT)
    blocks = blocks.reshape(2, ranks, cells, 2, share)
    coef = jnp.stack([blocks[0, :, :, 0] - blocks[1, :, :, 1], blocks[0, :, :, 1] + blocks[1, :, :, 0]])
    coef = jnp.where(live[None, :, :, None], coef, 0.0).astype(BF16)[:, :, :, None]
    coef = lax.all_to_all(coef, "tile", split_axis=2, concat_axis=3, tiled=True)
    coef = coef.reshape(2, ranks * cells, share)
    flat = receiver.reshape(2, ranks * cells, width)
    blocks = jnp.einsum("wgh,lgj->wlhj", coef, flat, preferred_element_type=F32)
    forward_data = jnp.stack([blocks[0, 0] - blocks[1, 1], blocks[1, 0] + blocks[0, 1]])
    masked = (forward_data * weights).astype(BF16)

    blocks = jnp.einsum("pks,qfs->pqkf", flat, masked, preferred_element_type=F32)
    back = jnp.stack([blocks[0, 0] + blocks[1, 1], blocks[0, 1] - blocks[1, 0]]).astype(BF16)
    back = back.reshape(2, ranks, 1, cells, share)
    back = lax.all_to_all(back, "tile", split_axis=3, concat_axis=2, tiled=True)
    back = jnp.where(live[None, :, :, None, None], back, jnp.zeros((), BF16)).reshape(2, ranks * cells, share)
    flat = source.reshape(2, ranks * cells, width)
    blocks = jnp.einsum("wgh,lgj->wlhj", back, flat, preferred_element_type=F32)
    adjoint = jnp.stack([blocks[0, 0] + blocks[1, 1], blocks[1, 0] - blocks[0, 1]])
    blocks = jnp.einsum(
        "pgs,qfs->pqgf", adjoint, focusing.astype(F32), precision=lax.Precision.HIGHEST, preferred_element_type=F32
    )
    corr = factor * jnp.stack([blocks[0, 0] + blocks[1, 1], blocks[1, 0] - blocks[0, 1]])
    return forward_data, adjoint, lax.psum(corr, "tile")


def solution(mesh):
    tiles, reps = mesh.shape["tile"], mesh.shape["rep"]
    short = tiles == 4 and reps == 4

    def per_device(*args):
        return (short_path if short else long_path)(*args)

    placed = (
        P(None, "grp", "tile"),
        P(None, "rep", "grp", "tile"),
        P(None, "rep", "grp", "tile"),
        P("grp", "tile"),
        P(("grp", "tile")),
    )
    return jax.shard_map(
        per_device,
        mesh=mesh,
        in_specs=placed,
        out_specs=(P(None, ("grp", "rep"), "tile"), P(None, ("grp", "rep"), "tile"), P(None, "rep", "grp")),
        check_vma=False,
    )
```

```python
import functools
import math

import jax
import jax.numpy as jnp
from jax import lax
from jax.experimental import pallas as pl
from jax.experimental.pallas import tpu as pltpu
from jax.sharding import PartitionSpec as P


SPAN = 256
BUCKET = 16
BF16 = jnp.bfloat16
F32 = jnp.float32

NT = (((1,), (1,)), ((), ()))
NN = (((1,), (0,)), ((), ()))
TN = (((0,), (0,)), ((), ()))


def dot(a, b, dims):
    return lax.dot_general(a, b, dims, preferred_element_type=F32)


def swap(x, step):
    count = lax.axis_size("rep")
    return lax.ppermute(x, "rep", [(i, i ^ step) for i in range(count)])


def cross(x, step, twist=0):
    reps = lax.axis_size("rep")
    count = lax.axis_size("tile") * reps
    pairs = [(i, i ^ (step * reps) ^ (twist if i % 2 else 0)) for i in range(count)]
    return lax.ppermute(x, ("tile", "rep"), pairs)


LANES = 128


def live_rows(ranks_ref, cell, shard, ranks):
    rows = lax.broadcasted_iota(jnp.int32, (ranks, 1), 0) + shard * ranks
    return rows < ranks_ref[pl.ds(cell, 1), pl.ds(0, 1)] * BUCKET


def fetch_kernel(ranks_in, *refs):
    count = (len(refs) - 3) // 2
    arrays, live_out, outs = refs[:count], refs[count], refs[count + 1 : 2 * count + 1]
    ranks_ref, sems = refs[2 * count + 1 :]
    scalars = pltpu.make_async_copy(ranks_in, ranks_ref, sems.at[count])
    copies = [pltpu.make_async_copy(ref, out, sems.at[i]) for i, (ref, out) in enumerate(zip(arrays, outs))]
    scalars.start()
    for copy in copies:
        copy.start()
    scalars.wait()
    for cell in range(ranks_in.shape[0]):
        live_out[pl.ds(cell, 1), :] = jnp.full((1, LANES), ranks_ref[cell], jnp.int32)
    for copy in copies:
        copy.wait()


def forward_kernel(ranks_ref, own_ref, pair_ref, lift_ref, foc_ref, *refs):
    ranks, tiles = own_ref.shape[1], own_ref.shape[2]
    outs, bundle, blocks = refs[:tiles], refs[tiles], refs[tiles + 1]
    here = lax.axis_index("tile")
    me = lax.axis_index("rep")
    core = lax.rem(me, 2)
    points = foc_ref.shape[0] // 2
    pieces = (own_ref, pair_ref)
    rows = [ref[part, :, cell, :] for cell in range(tiles) for ref in pieces for part in range(2)]
    prod = dot(jnp.concatenate(rows, axis=0), foc_ref[...], NT)
    for cell in range(tiles):
        for shard in range(2):
            mask = live_rows(ranks_ref, cell, me ^ shard, ranks)
            first = (cell * 2 + shard) * 2 * ranks
            real = prod[first : first + ranks]
            imag = prod[first + ranks : first + 2 * ranks]
            coef = [real[:, :points] - imag[:, points:], real[:, points:] + imag[:, :points]]
            for part in range(2):
                spot = pl.multiple_of(((core ^ shard) * 2 + part) * ranks, ranks)
                blocks[cell, pl.ds(spot, ranks), :] = jnp.where(mask, coef[part], 0.0).astype(BF16)
    for step in range(tiles):
        outs[step][...] = blocks[here ^ step]
    size = 2 * ranks
    bundle[pl.ds(0, size)] = lift_ref[...].reshape(size, tiles, points)
    bundle[pl.ds(size, size)] = own_ref[...].reshape(size, tiles, points)
    own = blocks[here, pl.ds(pl.multiple_of(core * size, size), size), :]
    bundle[pl.ds(2 * size, size // tiles)] = own.reshape(size // tiles, tiles, points)


def put_lift(out, spot, slot, real, imag):
    ranks, width = real.shape
    out[spot, slot, pl.ds(0, ranks), pl.ds(0, width)] = real
    out[spot, slot, pl.ds(0, ranks), pl.ds(width, width)] = imag
    out[spot, slot, pl.ds(ranks, ranks), pl.ds(0, width)] = -imag
    out[spot, slot, pl.ds(ranks, ranks), pl.ds(width, width)] = real


def lift_kernel(keep_ref, own_ref, pair_ref, far_ref, out, weight):
    ranks, tiles, width = own_ref.shape[1:]
    columns = lax.broadcasted_iota(jnp.int32, weight.shape, 1)
    columns = jnp.where(columns >= width, columns - width, columns)
    weight[...] = (columns < keep_ref[0]).astype(F32)
    here = lax.axis_index("tile")
    core = lax.rem(lax.axis_index("rep"), 2)
    for cell in range(tiles):
        spot = here ^ cell
        put_lift(out, spot, core, own_ref[0, :, cell, :], own_ref[1, :, cell, :])
        put_lift(out, spot, 1 - core, pair_ref[0, :, cell, :], pair_ref[1, :, cell, :])
        put_lift(out, spot, 2 + core, far_ref[pl.ds(0, ranks), cell, :], far_ref[pl.ds(ranks, ranks), cell, :])


def image_basis_kernel(ranks_ref, own_ref, pair_ref, far_ref, last_ref, out):
    ranks, tiles, width = own_ref.shape[1:]
    size = 2 * ranks
    here = lax.axis_index("tile")
    me = lax.axis_index("rep")
    core = lax.rem(me, 2)
    for cell in range(tiles):
        pieces = [(core, me, own_ref[0, :, cell, :], own_ref[1, :, cell, :])]
        pieces.append((1 - core, me ^ 1, pair_ref[0, :, cell, :], pair_ref[1, :, cell, :]))
        for slot, shard, ref in ((2 + core, me ^ 2, far_ref), (3 - core, me ^ 3, last_ref)):
            parts = [ref[pl.ds(size + part * ranks, ranks), cell, :] for part in range(2)]
            pieces.append((slot, shard, *parts))
        spot = here ^ cell
        for slot, shard, real, imag in pieces:
            mask = live_rows(ranks_ref, cell, shard, ranks)
            real = jnp.where(mask, real.astype(F32), 0.0)
            imag = jnp.where(mask, imag.astype(F32), 0.0)
            out[spot, slot, pl.ds(0, ranks), pl.ds(0, width)] = real.astype(BF16)
            out[spot, slot, pl.ds(0, ranks), pl.ds(width, width)] = (-imag).astype(BF16)
            out[spot, slot, pl.ds(ranks, ranks), pl.ds(0, width)] = imag.astype(BF16)
            out[spot, slot, pl.ds(ranks, ranks), pl.ds(width, width)] = real.astype(BF16)


def early_kernel(near_ref, far_ref, last_ref, mine_ref, lift_in, lift_ref, part_out, coef):
    tiles, reps, block, width2 = lift_ref.shape
    core = lax.rem(lax.axis_index("rep"), 2)
    here = lax.axis_index("tile")
    points = part_out.shape[0]
    ranks = block // 2
    for cell in range(tiles):
        put_lift(
            lift_ref, here ^ cell, 3 - core, last_ref[pl.ds(0, ranks), cell, :], last_ref[pl.ds(ranks, ranks), cell, :]
        )
    coef[pl.ds(0, 2)] = near_ref[...].reshape(2, block, points)
    coef[2 + core] = far_ref[pl.ds(2 * block, block // tiles)].reshape(block, points)
    coef[3 - core] = last_ref[pl.ds(2 * block, block // tiles)].reshape(block, points)
    rows = (tiles - 1) * 2 * block
    part = dot(coef[...].reshape(reps * block, points), lift_ref[0].reshape(reps * block, width2), TN)
    lift = lift_ref[pl.ds(1, tiles - 1), pl.ds(2 * core, 2)].reshape(rows, width2)
    part_out[...] = part + dot(mine_ref[...], lift, TN)


def middle_kernel(weight_ref, pair_ref, lift_ref, part_ref, *refs, factor):
    fwd_out, own_corr, own_back = refs[:3]
    tiles, reps, block, width2 = lift_ref.shape
    sends, whole, high = refs[3 : 2 + tiles], refs[2 + tiles], refs[3 + tiles]
    me = lax.axis_index("rep")
    core = lax.rem(me, 2)
    points = whole.shape[0]
    width = width2 // 2
    share = points // reps
    lift = lift_ref[pl.ds(1, tiles - 1), pl.ds(2 - 2 * core, 2)].reshape((tiles - 1) * 2 * block, width2)
    total = part_ref[...] + dot(pair_ref[...], lift, TN)
    small = total.astype(BF16)
    whole[...] = total
    high[pl.ds(0, points), :] = small
    high[pl.ds(points, points), :] = small
    first = pl.multiple_of(me * share, share)
    mine = whole[pl.ds(first, share), :]
    fwd_out[0] = mine[:, :width]
    fwd_out[1] = mine[:, width:]
    muted = (mine * weight_ref[pl.ds(0, 1), :]).astype(BF16)
    back = dot(muted, lift_ref[...].reshape(tiles * reps * block, width2), NT).astype(BF16)
    cell = reps * block
    turned = jnp.concatenate([muted[:, width:], -muted[:, :width]], axis=1)
    left = jnp.concatenate([muted, turned], axis=0)
    corr = dot(left, high[pl.ds(first, points), :], NT) * factor
    own_corr[...] = corr
    own_back[...] = back[:, :cell]
    mixed = (corr[:share, :share] + corr[share:, :share]).astype(BF16)
    rest = corr.astype(BF16)
    group = share * (cell - share) // points
    for step in range(1, tiles):
        out = sends[step - 1]
        piece = back[:, step * cell : (step + 1) * cell]
        out[pl.ds(0, 2 * share), :] = rest
        out[pl.ds(0, share), pl.ds(0, share)] = mixed
        out[pl.ds(share, share), pl.ds(0, share)] = piece[:, :share]
        for part in range(share // group):
            rows = piece[part * group : (part + 1) * group, share:]
            out[pl.ds(2 * share, group), pl.ds(part * share, share)] = rows


def final_kernel(own_corr, own_back, basis_ref, *refs):
    tiles, reps, block, width2 = basis_ref.shape
    arrived = refs[: tiles - 1]
    adj_out, corr_out, adj, corr, back, sems = refs[tiles - 1 :]
    share, cell = own_back.shape
    points = own_corr.shape[1]
    width = width2 // 2
    group = share * (cell - share) // points
    mixed = sum(got[pl.ds(0, share), pl.ds(0, share)].astype(F32) for got in arrived) * 0.5
    turned = mixed.T
    shift = lax.axis_index("rep") * share
    lanes = lax.broadcasted_iota(jnp.int32, (share, points), 1)
    for part, block_sum in enumerate((mixed + turned, mixed - turned)):
        rows = pl.ds(part * share, share)
        others = sum(got[rows, :].astype(F32) for got in arrived)
        padded = jnp.concatenate([block_sum, jnp.zeros((share, points - share), F32)], axis=1)
        total = own_corr[rows, :] + jnp.where(lanes < share, padded, others)
        corr[part] = pltpu.roll(total, shift, 1)
    second = pltpu.make_async_copy(corr, corr_out, sems.at[1])
    second.start()
    back[:, pl.ds(0, cell)] = own_back[...]
    for step, got in enumerate(arrived, 1):
        back[:, pl.ds(step * cell, share)] = got[pl.ds(share, share), pl.ds(0, share)]
        for part in range(share // group):
            rows = got[pl.ds(2 * share, group), pl.ds(part * share, share)]
            back[pl.ds(part * group, group), pl.ds(step * cell + share, cell - share)] = rows
    image = dot(back[...], basis_ref[...].reshape(tiles * reps * block, width2), NN)
    adj[0] = image[:, :width]
    adj[1] = image[:, width:]
    first = pltpu.make_async_copy(adj, adj_out, sems.at[0])
    first.start()
    first.wait()
    second.wait()


def call(kernel, ins, outs, scratch, args, aliases={}):
    vmem, smem = pl.BlockSpec(memory_space=pltpu.VMEM), pl.BlockSpec(memory_space=pltpu.SMEM)
    kinds = {"s": smem, "h": pl.BlockSpec(memory_space=pl.ANY), "p": vmem}
    args = [pltpu.with_memory_space_constraint(a, pltpu.VMEM) if k == "p" else a for k, a in zip(ins, args)]
    return pl.pallas_call(
        kernel,
        in_specs=[kinds[kind] for kind in ins],
        out_specs=[vmem if isinstance(out, pl.MemoryRef) else kinds["h"] for out in outs],
        out_shape=outs,
        scratch_shapes=scratch,
        input_output_aliases=aliases,
    )(*args)


def short_path(focusing, source, receiver, tile_ranks, keep_counts):
    tiles, reps = lax.axis_size("tile"), lax.axis_size("rep")
    ranks, width = source.shape[1], source.shape[3]
    points = focusing.shape[1]
    share = points // reps
    block = 2 * ranks
    factor = 1.0 / math.sqrt(SPAN * width * tiles)
    shaped, placed = jax.ShapeDtypeStruct, pltpu.VMEM
    order = sorted(range(1, tiles), reverse=True)

    source_pair = swap(source, 1)
    receiver_pair = swap(receiver, 1)
    live, source, receiver, foc = call(
        fetch_kernel,
        "hhhh",
        [
            placed((8, LANES), jnp.int32),
            placed(source.shape, BF16),
            placed(receiver.shape, BF16),
            placed((2 * points, width), BF16),
        ],
        [pltpu.SMEM((tiles,), jnp.int32), pltpu.SemaphoreType.DMA((4,))],
        (tile_ranks.reshape(tiles), source, receiver, focusing.reshape(2 * points, width)),
    )
    made = call(
        forward_kernel,
        "ppppp",
        [placed((2 * block, points), BF16)] * tiles + [placed((2 * block + block // tiles, tiles, points), BF16)],
        [pltpu.VMEM((tiles, 2 * block, points), BF16)],
        (live, source, source_pair, receiver, foc),
    )
    far = swap(made[tiles], 2)
    got = {step: cross(made[step], step, 2) for step in order}
    last = swap(far, 1)
    gathered = jnp.concatenate([got[step] for step in range(1, tiles)], axis=0)
    spread = swap(gathered, 1)
    lift, weight = call(
        lift_kernel,
        "sppp",
        [placed((tiles, reps, block, 2 * width), BF16), placed((8, 2 * width), F32)],
        [],
        (keep_counts, receiver, receiver_pair, far),
    )
    lift, part = call(
        early_kernel,
        "ppppp",
        [placed(lift.shape, BF16), placed((points, 2 * width), F32)],
        [pltpu.VMEM((reps, block, points), BF16)],
        (made[0], far, last, gathered, lift),
        {4: 0},
    )
    middle = call(
        functools.partial(middle_kernel, factor=factor),
        "pppp",
        [placed((2, share, width), F32), placed((2 * share, points), F32), placed((share, reps * block), BF16)]
        + [placed((2 * share + share * (reps * block - share) // points, points), BF16)] * (tiles - 1),
        [pltpu.VMEM((points, 2 * width), F32), pltpu.VMEM((2 * points, 2 * width), BF16)],
        (weight, spread, lift, part),
    )
    forward_data, own_corr, own_back = middle[:3]
    sent = {step: cross(middle[2 + step], step) for step in order}
    (basis,) = call(
        image_basis_kernel,
        "ppppp",
        [placed((tiles, reps, block, 2 * width), BF16)],
        [],
        (live, source, source_pair, far, last),
    )
    adjoint, corr = call(
        final_kernel,
        "p" * (tiles + 2),
        [shaped((2, share, width), F32), shaped((2, share, points), F32)],
        [
            pltpu.VMEM((2, share, width), F32),
            pltpu.VMEM((2, share, points), F32),
            pltpu.VMEM((share, tiles * reps * block), BF16),
            pltpu.SemaphoreType.DMA((2,)),
        ],
        (own_corr, own_back, basis, *[sent[step] for step in range(1, tiles)]),
    )
    return forward_data, adjoint, corr


def bucket_live(rank_column, ranks):
    return (lax.iota(jnp.int32, ranks) // BUCKET)[:, None] < rank_column[None, :]


def long_path(focusing, source_basis, receiver_basis, tile_ranks, keep_counts):
    width = focusing.shape[2]
    share = focusing.shape[1] // lax.axis_size("rep")
    weights = (lax.iota(jnp.int32, width) < keep_counts[0]).astype(F32)
    factor = 1.0 / math.sqrt(SPAN * width * lax.axis_size("tile"))
    source = lax.all_gather(source_basis, "rep", axis=1, tiled=True)
    receiver = lax.all_gather(receiver_basis, "rep", axis=1, tiled=True)
    focal = lax.dynamic_slice_in_dim(focusing, lax.axis_index("rep") * share, share, 1)
    ranks, cells = source.shape[1], source.shape[2]
    live = bucket_live(tile_ranks[:, 0], ranks)

    blocks = dot(source.reshape(-1, width), focal.reshape(-1, width), NT)
    blocks = blocks.reshape(2, ranks, cells, 2, share)
    coef = jnp.stack([blocks[0, :, :, 0] - blocks[1, :, :, 1], blocks[0, :, :, 1] + blocks[1, :, :, 0]])
    coef = jnp.where(live[None, :, :, None], coef, 0.0).astype(BF16)[:, :, :, None]
    coef = lax.all_to_all(coef, "tile", split_axis=2, concat_axis=3, tiled=True)
    coef = coef.reshape(2, ranks * cells, share)
    flat = receiver.reshape(2, ranks * cells, width)
    blocks = jnp.einsum("wgh,lgj->wlhj", coef, flat, preferred_element_type=F32)
    forward_data = jnp.stack([blocks[0, 0] - blocks[1, 1], blocks[1, 0] + blocks[0, 1]])
    masked = (forward_data * weights).astype(BF16)

    blocks = jnp.einsum("pks,qfs->pqkf", flat, masked, preferred_element_type=F32)
    back = jnp.stack([blocks[0, 0] + blocks[1, 1], blocks[0, 1] - blocks[1, 0]]).astype(BF16)
    back = back.reshape(2, ranks, 1, cells, share)
    back = lax.all_to_all(back, "tile", split_axis=3, concat_axis=2, tiled=True)
    back = jnp.where(live[None, :, :, None, None], back, jnp.zeros((), BF16)).reshape(2, ranks * cells, share)
    flat = source.reshape(2, ranks * cells, width)
    blocks = jnp.einsum("wgh,lgj->wlhj", back, flat, preferred_element_type=F32)
    adjoint = jnp.stack([blocks[0, 0] + blocks[1, 1], blocks[1, 0] - blocks[0, 1]])
    blocks = jnp.einsum(
        "pgs,qfs->pqgf", adjoint, focusing.astype(F32), precision=lax.Precision.HIGHEST, preferred_element_type=F32
    )
    corr = factor * jnp.stack([blocks[0, 0] + blocks[1, 1], blocks[1, 0] - blocks[0, 1]])
    return forward_data, adjoint, lax.psum(corr, "tile")


def solution(mesh):
    tiles, reps = mesh.shape["tile"], mesh.shape["rep"]
    short = tiles == 4 and reps == 4

    def per_device(*args):
        return (short_path if short else long_path)(*args)

    placed = (
        P(None, "grp", "tile"),
        P(None, "rep", "grp", "tile"),
        P(None, "rep", "grp", "tile"),
        P("grp", "tile"),
        P(("grp", "tile")),
    )
    return jax.shard_map(
        per_device,
        mesh=mesh,
        in_specs=placed,
        out_specs=(P(None, ("grp", "rep"), "tile"), P(None, ("grp", "rep"), "tile"), P(None, "rep", "grp")),
        check_vma=False,
    )
```
